512 devices in a mesh: grp: 16 (over y, x_hi, core), seq: 32 (over z, x_lo).
Axes of the slice: x: 4 (x_hi: 2, x_lo: 2; x = x_hi * 2 + x_lo), y: 4, z: 16, core: 2. Of those that a mesh axis runs over, the one named last changes fastest.
Arguments:
- tokens: bfloat16 [16, 4096, 1024], P('grp', 'seq'), may hold values from -40 to 40
- queries: bfloat16 [16, 4096, 512], P('grp', 'seq'), may hold values from -8 to 8
- keys: bfloat16 [16, 4096, 512], P('grp', 'seq'), may hold values from -8 to 8
- values: bfloat16 [16, 4096, 512], P('grp', 'seq'), may hold values from -6 to 6
- attn_mask: int32 [16, 32, 32], P('grp', 'seq'), may hold values from 0 to 1, as said below
- out_proj: bfloat16 [512, 1024], replicated, may hold values from -0.25 to 0.25
- norm_gain_vector: float32 [1024], replicated, may hold values from 0.5 to 1.5
- w1_packed: bfloat16 [32, 2, 128, 128], P('grp'), may hold values from -0.375 to 0.375
- w1_rows: int32 [32, 2], replicated, may hold values from 0 to 7, as said below
- w2_packed: bfloat16 [32, 2, 128, 128], P('grp'), may hold values from -0.1875 to 0.1875
- w2_cols: int32 [32, 2], replicated, may hold values from 0 to 7, as said below
- grad_out: bfloat16 [16, 4096, 1024], P('grp', 'seq'), may hold values from -6 to 6
Outputs:
- output: bfloat16 [16, 4096, 1024], P('grp', 'seq')
- grad_tokens: bfloat16 [16, 4096, 1024], P('grp', 'seq')
The draws below stay inside these ranges and needn't reach their ends.
Inputs may be any that keep to these rules, and one draw needn't show every extreme that they name: attn_mask[s, i, i] is 1 for every sheet s and block i. `w1_rows`: the 2 entries of a row are distinct. `w2_cols`: the 2 entries of a row are distinct.
All inputs are finite; a program needn't handle non-finite values.
Results may differ from the reference program's by a relative error of at most 0.0035.
The reference program's roundings to bfloat16 on the way count: a program that leaves them out, or rounds other values in their place, can miss the bound.
Values may be sent and summed in bfloat16 or wider, within the bound.
A program may use at most 64 MiB of HBM per device.

```python
import jax
import jax.numpy as jnp
from jax import lax

D = 1024
FF = 4096
HD = 64
HEADS = 8
BLK = 128
NNZ = 2
SHEETS = 16
SEQ = 4096
NBK = 32
FB = 32
DB = 8


def scales_of(key, count):
    return 10.0 ** jax.random.uniform(key, (count,), jnp.float32, -0.5, 0.5)


def draw_tokens(key, part):
    row_scale = scales_of(jax.random.fold_in(key, 21), SHEETS * SEQ).reshape(SHEETS, SEQ, 1)
    col_scale = scales_of(jax.random.fold_in(key, 22), D)
    base = jnp.clip(jax.random.normal(jax.random.fold_in(key, 24), (SHEETS, SEQ, D), jnp.float32), -4.0, 4.0)
    return (base * row_scale * col_scale).astype(jnp.bfloat16)


def draw_queries(key, part):
    shape = (SHEETS, SEQ, HEADS * HD)
    base = jnp.clip(jax.random.normal(jax.random.fold_in(key, 42), shape, jnp.float32), -6.0, 6.0)
    return base.astype(jnp.bfloat16)


def draw_keys(key, part):
    shape = (SHEETS, SEQ, HEADS * HD)
    base = jnp.clip(jax.random.normal(jax.random.fold_in(key, 52), shape, jnp.float32), -6.0, 6.0)
    return base.astype(jnp.bfloat16)


def draw_attn_mask(key, part):
    bits = jax.random.randint(jax.random.fold_in(key, 61), (SHEETS, NBK, NBK), 0, 2)
    diagonal = (jnp.arange(NBK)[:, None] == jnp.arange(NBK)[None, :]).astype(jnp.int32)
    return jnp.maximum(bits, diagonal[None]).astype(jnp.int32)


def distinct_blocks(key):
    scores = jax.random.randint(key, (FB, DB), 0, 1048576) * DB + jnp.arange(DB)[None, :]
    order = jnp.argsort(scores, axis=1, stable=True)
    return order[:, :NNZ].astype(jnp.int32)


def draw_w1_rows(key, part):
    return distinct_blocks(jax.random.fold_in(key, 71))


def draw_w2_cols(key, part):
    return distinct_blocks(jax.random.fold_in(key, 72))


def levels(stream_key, dims, cuts, low, largest):
    factor_of, own = 1.0, jax.random.fold_in(stream_key, 6)
    for dim, blocks in cuts:
        draws = jnp.exp(jax.random.uniform(jax.random.fold_in(own, dim), (blocks,), jnp.float32, low / len(cuts), largest / len(cuts)))
        factor_of = factor_of * jnp.repeat(draws, dims[dim] // blocks).reshape([-1 if axis == dim else 1 for axis in range(len(dims))])
    return factor_of


def normal_values(own_key, extent, deviation, limit, split=(), kind=jnp.bfloat16):
    gain = levels(own_key, extent, split, -0.22, 0.18) if split else 1.0
    values = jax.random.normal(own_key, extent, jnp.float32) * deviation * gain
    return jnp.minimum(jnp.maximum(values, -limit), limit).astype(kind)


def setup_inputs(seed: int = 0) -> dict:
    key_list = jax.random.split(jax.random.key(seed), 13)
    return {
        "tokens": draw_tokens(jax.random.fold_in(key_list[12], 71), 0),
        "queries": draw_queries(jax.random.fold_in(key_list[12], 71), 0),
        "keys": draw_keys(jax.random.fold_in(key_list[12], 71), 0),
        "values": normal_values(key_list[3], (SHEETS, SEQ, HEADS * HD), 1.0, 6.0, ((0, 16), (1, 32))),
        "attn_mask": draw_attn_mask(jax.random.fold_in(key_list[12], 71), 0),
        "out_proj": normal_values(key_list[5], (HEADS * HD, D), (HEADS * HD) ** -0.5, 0.25),
        "norm_gain_vector": jnp.clip(1.0 + 0.1 * jax.random.normal(key_list[6], (D,), jnp.float32), 0.5, 1.5),
        "w1_packed": normal_values(key_list[7], (FB, NNZ, BLK, BLK), (NNZ * BLK) ** -0.5, 0.375, ((0, 16),)),
        "w1_rows": draw_w1_rows(jax.random.fold_in(key_list[12], 71), 0),
        "w2_packed": normal_values(key_list[9], (FB, NNZ, BLK, BLK), (FF * NNZ // DB) ** -0.5, 0.1875, ((0, 16),)),
        "w2_cols": draw_w2_cols(jax.random.fold_in(key_list[12], 71), 0),
        "grad_out": normal_values(key_list[11], (SHEETS, SEQ, D), 1.0, 6.0, ((0, 16), (1, 32))),
    }


def gelu_slope(pre):
    return 0.5 * (1.0 + jax.scipy.special.erf(pre * 0.7071067811865476)) + pre * jnp.exp(-0.5 * pre * pre) * 0.3989422804014327

def expand_mask(mask):
    rows_blk, cols_blk = mask.shape
    wide = jnp.broadcast_to(mask[:, None, :, None], (rows_blk, BLK, cols_blk, BLK))
    return wide.reshape(rows_blk * BLK, cols_blk * BLK) > 0

def split_heads(array):
    return array.reshape(array.shape[0], HEADS, HD).transpose(1, 0, 2)

def join_heads(array):
    return array.transpose(1, 0, 2).reshape(array.shape[1], HEADS * HD)

def attend_forward(query, key_rows, value_rows, allowed):
    scale = HD ** (-0.5)

    def one_head(args):
        q_head, k_head, v_head = args
        scores = jnp.dot(q_head, k_head.T, preferred_element_type=jnp.float32) * scale
        scores = jnp.where(allowed, scores, -jnp.inf)
        top = lax.optimization_barrier(jnp.max(scores, axis=1, keepdims=True))
        weight = jnp.exp(scores - top)
        total = lax.optimization_barrier(jnp.sum(weight, axis=1, keepdims=True))
        prob = (weight / total).astype(jnp.bfloat16)
        return jnp.dot(prob, v_head, preferred_element_type=jnp.float32)
    heads_out = lax.map(one_head, (split_heads(query), split_heads(key_rows), split_heads(value_rows)))
    return join_heads(heads_out).astype(jnp.bfloat16)

def layer_norm_forward(hidden_state, gain_vector):
    mean_row = lax.optimization_barrier(jnp.mean(hidden_state, axis=1, keepdims=True))
    mean_removed = hidden_state - mean_row
    reciprocal_deviation = lax.rsqrt(lax.optimization_barrier(jnp.mean(mean_removed * mean_removed, axis=1, keepdims=True)) + 1e-06)
    unit_rows = mean_removed * reciprocal_deviation
    return (unit_rows, reciprocal_deviation, (unit_rows * gain_vector).astype(jnp.bfloat16))

def layer_norm_backward(normed_gradient, gain_vector, unit_rows, reciprocal_deviation, gradient_rows):
    unit_gradient = normed_gradient * gain_vector
    inner_product = unit_gradient - lax.optimization_barrier(jnp.mean(unit_gradient, axis=1, keepdims=True)) - unit_rows * lax.optimization_barrier(jnp.mean(unit_gradient * unit_rows, axis=1, keepdims=True))
    return (gradient_rows.astype(jnp.float32) + reciprocal_deviation * inner_product).astype(jnp.bfloat16)

def dense_first(w1_packed, w1_rows):
    blocks = FF // BLK
    col_index = jnp.arange(blocks, dtype=jnp.int32)[:, None]
    full = jnp.zeros((D // BLK, BLK, blocks, BLK), w1_packed.dtype)
    full = full.at[w1_rows, :, col_index, :].set(w1_packed)
    return full.reshape(D, FF)

def dense_second(w2_packed, w2_cols):
    blocks = FF // BLK
    row_index = jnp.arange(blocks, dtype=jnp.int32)[:, None]
    full = jnp.zeros((blocks, BLK, D // BLK, BLK), w2_packed.dtype)
    full = full.at[row_index, :, w2_cols, :].set(w2_packed)
    return full.reshape(FF, D)

def reference(tokens, queries, keys, values, attn_mask, out_proj, norm_gain_vector, w1_packed, w1_rows, w2_packed, w2_cols, grad_out):
    first = dense_first(w1_packed, w1_rows)
    second = dense_second(w2_packed, w2_cols)

    def one_sheet(args):
        rows_in, query, key_rows, value_rows, mask, gradient_rows = args
        allowed = expand_mask(mask)
        attn = attend_forward(query, key_rows, value_rows, allowed)
        hidden_state = rows_in.astype(jnp.float32) + jnp.dot(attn, out_proj, preferred_element_type=jnp.float32)
        unit_rows, reciprocal_deviation, normed_rows = layer_norm_forward(hidden_state, norm_gain_vector)
        pre = jnp.dot(normed_rows, first, preferred_element_type=jnp.float32)
        act = jax.nn.gelu(pre, approximate=False).astype(jnp.bfloat16)
        mlp = jnp.dot(act, second, preferred_element_type=jnp.float32)
        result = (hidden_state + mlp).astype(jnp.bfloat16)
        dact = jnp.dot(gradient_rows, second.T, preferred_element_type=jnp.float32)
        dpre = (dact * gelu_slope(pre)).astype(jnp.bfloat16)
        normed_gradient = jnp.dot(dpre, first.T, preferred_element_type=jnp.float32)
        incoming_gradient_rows = layer_norm_backward(normed_gradient, norm_gain_vector, unit_rows, reciprocal_deviation, gradient_rows)
        return (result, incoming_gradient_rows)
    output, grad_tokens = lax.map(one_sheet, (tokens, queries, keys, values, attn_mask, grad_out))
    return (output, grad_tokens)
```

```python
import functools

import jax
import jax.numpy as jnp
from jax import lax
from jax.experimental import pallas as pl
from jax.experimental.pallas import tpu as pltpu
from jax.sharding import PartitionSpec as P

D = 1024
HD = 64
HEADS = 8
BLK = 128
HALF = 256
LOCAL_HEADS = 4
NEG = -1e30
BF16 = jnp.bfloat16
F32 = jnp.float32

NT = (((1,), (1,)), ((), ()))


def gather_attend_kernel(
    nz,
    ny,
    q_hbm,
    k_hbm,
    v_hbm,
    mask_ref,
    w1_hbm,
    w2_hbm,
    attn_ref,
    w1_all,
    w2_all,
    kv,
    give,
    qb,
    qgive,
    wown,
    bias,
    qz,
    top,
    total,
    acc,
    ogive,
    oin,
    loc,
    kv_send,
    kv_recv,
    x_send,
    x_recv,
    y_send,
    y_recv,
    yy_send,
    yy_recv,
    wx_send,
    wx_recv,
    wc_send,
    wc_recv,
):
    grp = lax.axis_index("grp")
    seq = lax.axis_index("seq")
    z = seq // 2
    xl = seq % 2
    y = grp // 4
    xh = (grp // 2) % 2
    core = grp % 2
    half = nz // 2

    def seq_dev(zz, xx):
        return {"grp": grp, "seq": zz * 2 + xx}

    def grp_index(yy, hh, cc):
        return (yy * 2 + hh) * 2 + cc

    z_next = (z + 1) % nz
    z_prev = (z + nz - 1) % nz
    y_next = (y + 1) % ny
    y_prev = (y + ny - 1) % ny
    y_far = (y + 2) % ny
    dev_r = seq_dev(z_next, xl)
    dev_l = seq_dev(z_prev, xl)
    dev_p = seq_dev(z, 1 - xl)
    dev_yn = {"grp": grp_index(y_next, xh, core), "seq": seq}
    dev_yp = {"grp": grp_index(y_prev, xh, core), "seq": seq}
    dev_xo = {"grp": grp_index(y, 1 - xh, core), "seq": z * 2 + 1 - xl}
    dev_co = {"grp": grp_index(y, xh, 1 - core), "seq": seq}

    mine = pl.ds(pl.multiple_of(xl * HALF, HALF), HALF)
    other = pl.ds(pl.multiple_of((1 - xl) * HALF, HALF), HALF)

    w_hbm = (w1_hbm, w2_hbm)
    w_all = (w1_all, w2_all)

    def local(i):
        pairs = (
            (k_hbm.at[:, mine], kv.at[z, 0, 0]),
            (v_hbm.at[:, mine], kv.at[z, 0, 1]),
            (k_hbm.at[:, other], give.at[0]),
            (v_hbm.at[:, other], give.at[1]),
            (q_hbm.at[:, mine], qb.at[0]),
            (q_hbm.at[:, other], qgive),
            (w1_hbm, wown.at[0]),
            (w2_hbm, wown.at[1]),
            (wown.at[0], w1_all.at[pl.ds(2 * grp, 2)]),
            (wown.at[1], w2_all.at[pl.ds(2 * grp, 2)]),
        )
        return pltpu.make_async_copy(pairs[i][0], pairs[i][1], loc.at[i])

    def remote(src, dst, send, recv, device):
        return pltpu.make_async_remote_copy(
            src_ref=src,
            dst_ref=dst,
            send_sem=send,
            recv_sem=recv,
            device_id=device,
            device_id_type=pl.DeviceIdType.MESH,
        )

    for i in range(8):
        local(i).start()

    rows = lax.broadcasted_iota(jnp.int32, (32, 32), 0)
    cols = lax.broadcasted_iota(jnp.int32, (32, 32), 1)
    seen = jnp.broadcast_to(mask_ref[...].astype(F32), (32, 32))
    seen = jnp.sum(jnp.where(rows == cols, seen, 0.0), axis=1, keepdims=True)
    bias[0] = jnp.broadcast_to(jnp.where(seen == 1.0, 0.0, NEG), (32, BLK))

    barrier = pltpu.get_barrier_semaphore()
    for device in (dev_r, dev_l, dev_p, dev_yn, dev_yp, dev_xo, dev_co):
        pl.semaphore_signal(
            barrier, inc=1, device_id=device, device_id_type=pl.DeviceIdType.MESH
        )
    pl.semaphore_wait(barrier, 7)

    def kv_copy(direction, d, j):
        slot = (z + nz - d) % nz if direction == 0 else (z + d) % nz
        return remote(
            kv.at[slot, j],
            kv.at[slot, j],
            kv_send.at[direction, d, j],
            kv_recv.at[direction, d, j],
            dev_r if direction == 0 else dev_l,
        )

    def kv_landed(direction, d, j):
        slot = (z + nz - d) % nz if direction == 0 else (z + d) % nz
        return remote(
            kv.at[slot, j],
            kv.at[slot, j],
            kv_send.at[direction, d - 1, j],
            kv_recv.at[direction, d - 1, j],
            dev_r if direction == 0 else dev_l,
        )

    def w_slot(t, g):
        return w_all[t].at[pl.ds(2 * g, 2)]

    def y_copy(direction, t):
        return remote(
            wown.at[t],
            w_slot(t, grp),
            y_send.at[direction, t],
            y_recv.at[direction, t],
            dev_yn if direction == 0 else dev_yp,
        )

    def yy_copy(t):
        g = grp_index(y_prev if t == 0 else y_next, xh, core)
        return remote(
            w_slot(t, g),
            w_slot(t, g),
            yy_send.at[t],
            yy_recv.at[t],
            dev_yn if t == 0 else dev_yp,
        )

    y_of = (y, y_prev, y_next, y_far)

    def wx_copy(i, t):
        g = grp_index(y_of[i], xh, core)
        return remote(
            wown.at[t] if i == 0 else w_slot(t, g),
            w_slot(t, g),
            wx_send.at[i, t],
            wx_recv.at[i, t],
            dev_xo,
        )

    def wc_copy(i, t):
        g = grp_index(y_of[i % 4], xh if i < 4 else 1 - xh, core)
        return remote(
            wown.at[t] if i == 0 else w_slot(t, g),
            w_slot(t, g),
            wc_send.at[i, t],
            wc_recv.at[i, t],
            dev_co,
        )

    x_pairs = (
        (give, kv.at[z, 1]),
        (qgive, qb.at[1]),
        (bias.at[0], bias.at[1]),
        (ogive, oin),
    )

    def x_copy(i):
        return remote(x_pairs[i][0], x_pairs[i][1], x_send.at[i], x_recv.at[i], dev_p)

    local(2).wait()
    local(3).wait()
    x_copy(0).start()
    local(0).wait()
    local(1).wait()
    kv_copy(0, 0, 0).start()
    kv_copy(1, 0, 0).start()
    local(5).wait()
    x_copy(1).start()
    x_copy(2).start()
    local(6).wait()
    local(7).wait()
    for t in range(2):
        y_copy(0, t).start()
        y_copy(1, t).start()
        wx_copy(0, t).start()
        wc_copy(0, t).start()
        local(8 + t).start()
    x_copy(0).wait_recv()
    kv_copy(0, 0, 1).start()
    kv_copy(1, 0, 1).start()
    local(4).wait()
    x_copy(1).wait_recv()
    x_copy(2).wait_recv()

    lane = lax.broadcasted_iota(jnp.int32, (2 * BLK, BLK), 1)
    for h in range(LOCAL_HEADS):
        pair = pl.ds((h // 2) * BLK, BLK)
        both = jnp.concatenate([qb[0, :, pair], qb[1, :, pair]], axis=0).astype(F32)
        keep = (lane < HD) if h % 2 == 0 else (lane >= HD)
        qz[h] = jnp.where(keep, both * (HD**-0.5), 0.0).astype(BF16)
    top[...] = jnp.full(top.shape, NEG, F32)
    total[...] = jnp.zeros(total.shape, F32)
    acc[...] = jnp.zeros(acc.shape, F32)

    def attend(slot, p):
        pair = pl.ds(p * BLK, BLK)
        keys = jnp.concatenate([kv[slot, 0, 0, :, pair], kv[slot, 1, 0, :, pair]], axis=0)
        vals = jnp.concatenate([kv[slot, 0, 1, :, pair], kv[slot, 1, 1, :, pair]], axis=0)
        vals_t = jnp.transpose(vals)
        shift = []
        for j in range(2):
            block = slot * 2 + (xl if j == 0 else 1 - xl)
            shift.append(
                jnp.concatenate(
                    [bias[0, pl.ds(block, 1), :], bias[1, pl.ds(block, 1), :]], axis=1
                )
            )
        for u in range(2):
            h = 2 * p + u
            s = lax.dot_general(keys, qz[h], NT, preferred_element_type=F32)
            s0, s1 = s[:BLK], s[BLK:]
            old = top[h]
            new = jnp.maximum(
                jnp.max(s0, axis=0, keepdims=True) + shift[0],
                jnp.max(s1, axis=0, keepdims=True) + shift[1],
            )
            new = jnp.maximum(old, new)
            fade = jnp.exp(old - new)
            p0 = jnp.exp(s0 - (new - shift[0]))
            p1 = jnp.exp(s1 - (new - shift[1]))
            total[h] = (
                fade * total[h]
                + jnp.sum(p0, axis=0, keepdims=True)
                + jnp.sum(p1, axis=0, keepdims=True)
            )
            weight = jnp.concatenate([p0, p1], axis=0).astype(BF16)
            part = jnp.dot(
                vals_t[u * HD : (u + 1) * HD], weight, preferred_element_type=F32
            )
            acc[h] = acc[h] * fade + part
            top[h] = new

    def w_first():
        for t in range(2):
            y_copy(0, t).wait_recv()
            y_copy(1, t).wait_recv()
        yy_copy(0).start()
        yy_copy(1).start()
        for i in (1, 2):
            for t in range(2):
                wx_copy(i, t).start()
                wc_copy(i, t).start()

    def w_second():
        for t in range(2):
            yy_copy(t).wait_recv()
            wx_copy(3, t).start()
            wc_copy(3, t).start()
        for t in range(2):
            wx_copy(0, t).wait_recv()
            wc_copy(4, t).start()

    def w_third():
        for i in (1, 2):
            for t in range(2):
                wx_copy(i, t).wait_recv()
                wc_copy(4 + i, t).start()

    def w_fourth():
        for t in range(2):
            wx_copy(3, t).wait_recv()
            wc_copy(7, t).start()

    def step(d, carry):
        back = (z + nz - (d - 1)) % nz
        ahead = (z + d - 1) % nz
        inner = d < half

        kv_landed(0, d, 0).wait_recv()

        @pl.when(inner)
        def _():
            kv_copy(0, d, 0).start()

        attend(back, 0)

        @pl.when(inner)
        def _():
            kv_landed(1, d, 0).wait_recv()

        @pl.when(d < half - 1)
        def _():
            kv_copy(1, d, 0).start()

        attend(back, 1)

        @pl.when(inner)
        def _():
            kv_landed(0, d, 1).wait_recv()

        @pl.when(d < half - 1)
        def _():
            kv_copy(0, d, 1).start()

        @pl.when(d > 1)
        def _():
            attend(ahead, 0)

        kv_landed(1, d, 1).wait_recv()

        @pl.when(inner)
        def _():
            kv_copy(1, d, 1).start()

        @pl.when(d > 1)
        def _():
            attend(ahead, 1)

        pl.when(d == 1)(w_first)
        pl.when(d == 2)(w_second)
        pl.when(d == 4)(w_third)
        pl.when(d == 5)(w_fourth)
        return carry

    lax.fori_loop(1, half + 1, step, 0)
    far = (z + half) % nz
    attend(far, 0)
    attend(far, 1)

    heads_out = jnp.concatenate(
        [acc[h] / total[h] for h in range(LOCAL_HEADS)], axis=0
    )
    heads_out = jnp.transpose(heads_out).astype(BF16)
    ogive[...] = heads_out[BLK:]
    attn_ref[:, mine] = heads_out[:BLK]
    x_copy(3).start()

    for i in range(8):
        for t in range(2):
            wc_copy(i, t).wait_recv()
    for t in range(2):
        local(8 + t).wait()
        y_copy(0, t).wait_send()
        y_copy(1, t).wait_send()
        yy_copy(t).wait_send()
        for i in range(4):
            wx_copy(i, t).wait_send()
        for i in range(8):
            wc_copy(i, t).wait_send()

    def drain(d, carry):
        kv_copy(0, d, 0).wait_send()
        kv_copy(1, d, 1).wait_send()

        @pl.when(d < half - 1)
        def _():
            kv_copy(0, d, 1).wait_send()
            kv_copy(1, d, 0).wait_send()

        return carry

    lax.fori_loop(0, half, drain, 0)
    for i in range(3):
        x_copy(i).wait_send()
    x_copy(3).wait()
    attn_ref[:, other] = oin[...]


def gather_attend(nz, ny, query, key, value, mask, w1, w2):
    any_spec = pl.BlockSpec(memory_space=pl.ANY)
    vmem_spec = pl.BlockSpec(memory_space=pltpu.VMEM)
    half = nz // 2
    dma = pltpu.SemaphoreType.DMA
    fb = w1.shape[0] * ny * 4
    return pl.pallas_call(
        functools.partial(gather_attend_kernel, nz, ny),
        name="gather_attend",
        out_shape=(
            jax.ShapeDtypeStruct(query.shape, BF16),
            jax.ShapeDtypeStruct((fb,) + w1.shape[1:], BF16),
            jax.ShapeDtypeStruct((fb,) + w2.shape[1:], BF16),
        ),
        in_specs=[any_spec, any_spec, any_spec, vmem_spec, any_spec, any_spec],
        out_specs=(vmem_spec, any_spec, any_spec),
        scratch_shapes=[
            pltpu.VMEM((nz, 2, 2, BLK, HALF), BF16),
            pltpu.VMEM((2, BLK, HALF), BF16),
            pltpu.VMEM((2, BLK, HALF), BF16),
            pltpu.VMEM((BLK, HALF), BF16),
            pltpu.VMEM((2,) + w1.shape, BF16),
            pltpu.VMEM((2, 32, BLK), F32),
            pltpu.VMEM((LOCAL_HEADS, 2 * BLK, BLK), BF16),
            pltpu.VMEM((LOCAL_HEADS, 1, 2 * BLK), F32),
            pltpu.VMEM((LOCAL_HEADS, 1, 2 * BLK), F32),
            pltpu.VMEM((LOCAL_HEADS, HD, 2 * BLK), F32),
            pltpu.VMEM((BLK, HALF), BF16),
            pltpu.VMEM((BLK, HALF), BF16),
            dma((10,)),
            dma((2, half, 2)),
            dma((2, half, 2)),
            dma((4,)),
            dma((4,)),
            dma((2, 2)),
            dma((2, 2)),
            dma((2,)),
            dma((2,)),
            dma((4, 2)),
            dma((4, 2)),
            dma((8, 2)),
            dma((8, 2)),
        ],
        compiler_params=pltpu.CompilerParams(
            collective_id=0, has_side_effects=True, vmem_limit_bytes=24 << 20
        ),
    )(query, key, value, mask, w1, w2)


def mlp_kernel(
    rows_ref,
    cols_ref,
    tokens_hbm,
    attn_hbm,
    proj_hbm,
    gain_ref,
    w1_hbm,
    w2_hbm,
    grad_hbm,
    out_ref,
    gin_ref,
    tokens,
    attn,
    proj,
    w1,
    w2,
    grad,
    normed,
    gblk,
    xhat,
    mlp_acc,
    dn_acc,
    act,
    dpre,
    sems,
):
    copies = [
        pltpu.make_async_copy(src, dst, sems.at[i])
        for i, (src, dst) in enumerate(
            (
                (attn_hbm, attn),
                (proj_hbm, proj),
                (tokens_hbm, tokens),
                (grad_hbm, grad),
                (w1_hbm, w1),
                (w2_hbm, w2),
            )
        )
    ]
    for copy in copies:
        copy.start()
    for copy in copies[:3]:
        copy.wait()
    hidden = tokens[...].astype(F32) + jnp.dot(
        attn[...], proj[...], preferred_element_type=F32
    )
    mean = jnp.mean(hidden, axis=1, keepdims=True)
    removed = hidden - mean
    rstd = lax.rsqrt(jnp.mean(removed * removed, axis=1, keepdims=True) + 1e-06)
    unit = removed * rstd
    xhat[...] = unit
    normed_rows = (unit * gain_ref[...]).astype(BF16)
    db = D // BLK
    for b in range(db):
        cut = slice(b * BLK, (b + 1) * BLK)
        normed[b] = normed_rows[:, cut]
        mlp_acc[b] = hidden[:, cut]
        dn_acc[b] = jnp.zeros((BLK, BLK), F32)
    copies[3].wait()
    for b in range(db):
        gblk[b] = grad[:, b * BLK : (b + 1) * BLK]
    copies[4].wait()
    copies[5].wait()

    fb = w1.shape[0]
    group = 4

    def first(i, carry):
        for u in range(group):
            c = i * group + u
            r0, r1 = rows_ref[c, 0], rows_ref[c, 1]
            c0, c1 = cols_ref[c, 0], cols_ref[c, 1]
            picked = jnp.concatenate([normed[r0], normed[r1]], axis=1)
            pre = jnp.dot(
                picked, w1[c].reshape(2 * BLK, BLK), preferred_element_type=F32
            )
            gsel = jnp.concatenate([gblk[c0], gblk[c1]], axis=1)
            w2c = jnp.concatenate([w2[c, 0], w2[c, 1]], axis=1)
            dact = lax.dot_general(gsel, w2c, NT, preferred_element_type=F32)
            phi = 0.5 * (1.0 + lax.erf(pre * 0.7071067811865476))
            act[c] = (pre * phi).astype(BF16)
            slope = phi + pre * jnp.exp(-0.5 * pre * pre) * 0.3989422804014327
            dpre[c] = (dact * slope).astype(BF16)
        return carry

    lax.fori_loop(0, fb // group, first, 0)

    def second(i, carry):
        for u in range(group):
            c = i * group + u
            r0, r1 = rows_ref[c, 0], rows_ref[c, 1]
            c0, c1 = cols_ref[c, 0], cols_ref[c, 1]
            w2c = jnp.concatenate([w2[c, 0], w2[c, 1]], axis=1)
            fpart = jnp.dot(act[c], w2c, preferred_element_type=F32)
            mlp_acc[c0] += fpart[:, :BLK]
            mlp_acc[c1] += fpart[:, BLK:]
            bpart = lax.dot_general(
                dpre[c], w1[c].reshape(2 * BLK, BLK), NT, preferred_element_type=F32
            )
            dn_acc[r0] += bpart[:, :BLK]
            dn_acc[r1] += bpart[:, BLK:]
        return carry

    lax.fori_loop(0, fb // group, second, 0)

    for b in range(db):
        out_ref[:, b * BLK : (b + 1) * BLK] = mlp_acc[b].astype(BF16)
    dx = jnp.concatenate([dn_acc[b] for b in range(db)], axis=1) * gain_ref[...]
    unit = xhat[...]
    inner = (
        dx
        - jnp.mean(dx, axis=1, keepdims=True)
        - unit * jnp.mean(dx * unit, axis=1, keepdims=True)
    )
    gin_ref[...] = (grad[...].astype(F32) + rstd * inner).astype(BF16)


def mlp_layer(rows, cols, tokens, attn, proj, gain, w1, w2, grad):
    any_spec = pl.BlockSpec(memory_space=pl.ANY)
    vmem_spec = pl.BlockSpec(memory_space=pltpu.VMEM)
    smem_spec = pl.BlockSpec(memory_space=pltpu.SMEM)
    db = D // BLK
    fb = w1.shape[0]
    out = jax.ShapeDtypeStruct(tokens.shape, BF16)
    return pl.pallas_call(
        mlp_kernel,
        name="mlp_layer",
        out_shape=(out, out),
        in_specs=[
            smem_spec,
            smem_spec,
            any_spec,
            any_spec,
            any_spec,
            vmem_spec,
            any_spec,
            any_spec,
            any_spec,
        ],
        out_specs=(vmem_spec, vmem_spec),
        scratch_shapes=[
            pltpu.VMEM(tokens.shape, BF16),
            pltpu.VMEM(attn.shape, BF16),
            pltpu.VMEM(proj.shape, BF16),
            pltpu.VMEM(w1.shape, BF16),
            pltpu.VMEM(w2.shape, BF16),
            pltpu.VMEM(grad.shape, BF16),
            pltpu.VMEM((db, BLK, BLK), BF16),
            pltpu.VMEM((db, BLK, BLK), BF16),
            pltpu.VMEM(tokens.shape, F32),
            pltpu.VMEM((db, BLK, BLK), F32),
            pltpu.VMEM((db, BLK, BLK), F32),
            pltpu.VMEM((fb, BLK, BLK), BF16),
            pltpu.VMEM((fb, BLK, BLK), BF16),
            pltpu.SemaphoreType.DMA((6,)),
        ],
        compiler_params=pltpu.CompilerParams(vmem_limit_bytes=24 << 20),
    )(rows, cols, tokens, attn, proj, gain, w1, w2, grad)


def body(
    nz,
    ny,
    tokens,
    queries,
    keys,
    values,
    attn_mask,
    out_proj,
    norm_gain_vector,
    w1_packed,
    w1_rows,
    w2_packed,
    w2_cols,
    grad_out,
):
    attn, w1_all, w2_all = gather_attend(
        nz, ny, queries[0], keys[0], values[0], attn_mask[0], w1_packed, w2_packed
    )
    out, gin = mlp_layer(
        w1_rows,
        w2_cols,
        tokens[0],
        attn,
        out_proj,
        norm_gain_vector.reshape(1, D),
        w1_all,
        w2_all,
        grad_out[0],
    )
    return (out[None], gin[None])


def solution(mesh):
    nz = mesh.shape["seq"] // 2
    ny = mesh.shape["grp"] // 4
    return jax.shard_map(
        functools.partial(body, nz, ny),
        mesh=mesh,
        in_specs=(
            P("grp", "seq", None),
            P("grp", "seq", None),
            P("grp", "seq", None),
            P("grp", "seq", None),
            P("grp", "seq", None),
            P(),
            P(),
            P("grp", None, None, None),
            P(),
            P("grp", None, None, None),
            P(),
            P("grp", "seq", None),
        ),
        out_specs=(P("grp", "seq", None), P("grp", "seq", None)),
        check_vma=False,
    )
```

```python
import functools

import jax
import jax.numpy as jnp
from jax import lax
from jax.experimental import pallas as pl
from jax.experimental.pallas import tpu as pltpu
from jax.sharding import PartitionSpec as P

D = 1024
HD = 64
HEADS = 8
BLK = 128
HALF = 256
LOCAL_HEADS = 4
NEG = -1e30
BF16 = jnp.bfloat16
F32 = jnp.float32

NT = (((1,), (1,)), ((), ()))


def gather_attend_kernel(
    nz,
    ny,
    cols_hbm,
    q_hbm,
    k_hbm,
    v_hbm,
    mask_hbm,
    w1_hbm,
    w2_hbm,
    tokens_hbm,
    proj_hbm,
    gain_hbm,
    grad_hbm,
    hidden_ref,
    dact_ref,
    gblk,
    gain_ref,
    w1_all,
    w2_all,
    kv,
    give,
    qb,
    qgive,
    wown,
    cols_ref,
    mask,
    tokens,
    proj,
    bias,
    qz,
    top,
    total,
    acc,
    okeep,
    ogive,
    oin,
    loc,
    kv_send,
    kv_recv,
    x_send,
    x_recv,
    y_send,
    y_recv,
    yy_send,
    yy_recv,
    wx_send,
    wx_recv,
    wc_send,
    wc_recv,
):
    grp = lax.axis_index("grp")
    seq = lax.axis_index("seq")
    z = seq // 2
    xl = seq % 2
    y = grp // 4
    xh = (grp // 2) % 2
    core = grp % 2
    half = nz // 2
    db = D // BLK

    def seq_dev(zz, xx):
        return {"grp": grp, "seq": zz * 2 + xx}

    def grp_index(yy, hh, cc):
        return (yy * 2 + hh) * 2 + cc

    z_next = (z + 1) % nz
    z_prev = (z + nz - 1) % nz
    y_next = (y + 1) % ny
    y_prev = (y + ny - 1) % ny
    y_far = (y + 2) % ny
    dev_r = seq_dev(z_next, xl)
    dev_l = seq_dev(z_prev, xl)
    dev_p = seq_dev(z, 1 - xl)
    dev_yn = {"grp": grp_index(y_next, xh, core), "seq": seq}
    dev_yp = {"grp": grp_index(y_prev, xh, core), "seq": seq}
    dev_xo = {"grp": grp_index(y, 1 - xh, core), "seq": z * 2 + 1 - xl}
    dev_co = {"grp": grp_index(y, xh, 1 - core), "seq": seq}

    def columns(side, p):
        return pl.ds(pl.multiple_of(side * HALF + p * BLK, BLK), BLK)

    w_all = (w1_all, w2_all)

    pairs = []
    for p in range(2):
        pairs += [
            (k_hbm.at[:, columns(xl, p)], kv.at[p, z, 0, 0]),
            (v_hbm.at[:, columns(xl, p)], kv.at[p, z, 0, 1]),
            (k_hbm.at[:, columns(1 - xl, p)], give.at[p, 0]),
            (v_hbm.at[:, columns(1 - xl, p)], give.at[p, 1]),
            (q_hbm.at[:, columns(xl, p)], qb.at[0, p]),
            (q_hbm.at[:, columns(1 - xl, p)], qgive.at[p]),
        ]
    pairs += [
        (mask_hbm, mask),
        (w1_hbm, wown.at[0]),
        (w2_hbm, wown.at[1]),
        (wown.at[0], w1_all.at[pl.ds(2 * grp, 2)]),
        (wown.at[1], w2_all.at[pl.ds(2 * grp, 2)]),
        (proj_hbm, proj),
        (tokens_hbm, tokens),
        (gain_hbm, gain_ref),
        (cols_hbm, cols_ref),
    ]
    for b in range(db):
        pairs.append((grad_hbm.at[:, b * BLK : (b + 1) * BLK], gblk.at[b]))

    def local(i):
        return pltpu.make_async_copy(pairs[i][0], pairs[i][1], loc.at[i])

    def remote(src, dst, send, recv, device):
        return pltpu.make_async_remote_copy(
            src_ref=src,
            dst_ref=dst,
            send_sem=send,
            recv_sem=recv,
            device_id=device,
            device_id_type=pl.DeviceIdType.MESH,
        )

    for i in range(15):
        local(i).start()

    barrier = pltpu.get_barrier_semaphore()
    for device in (dev_r, dev_l, dev_p, dev_yn, dev_yp, dev_xo, dev_co):
        pl.semaphore_signal(
            barrier, inc=1, device_id=device, device_id_type=pl.DeviceIdType.MESH
        )

    local(12).wait()
    rows = lax.broadcasted_iota(jnp.int32, (32, 32), 0)
    cols = lax.broadcasted_iota(jnp.int32, (32, 32), 1)
    seen = jnp.broadcast_to(mask[...].astype(F32), (32, 32))
    seen = jnp.sum(jnp.where(rows == cols, seen, 0.0), axis=1, keepdims=True)
    bias[0] = jnp.broadcast_to(jnp.where(seen == 1.0, 0.0, NEG), (32, BLK))
    pl.semaphore_wait(barrier, 7)

    def kv_slot(direction, d):
        return (z + nz - d) % nz if direction == 0 else (z + d) % nz

    def kv_copy(direction, p, d, j):
        here = kv.at[p, kv_slot(direction, d), j]
        return remote(
            here,
            here,
            kv_send.at[direction, p, d, j],
            kv_recv.at[direction, p, d, j],
            dev_r if direction == 0 else dev_l,
        )

    def kv_landed(direction, p, d, j):
        here = kv.at[p, kv_slot(direction, d), j]
        return remote(
            here,
            here,
            kv_send.at[direction, p, d - 1, j],
            kv_recv.at[direction, p, d - 1, j],
            dev_r if direction == 0 else dev_l,
        )

    def w_slot(t, g):
        return w_all[t].at[pl.ds(2 * g, 2)]

    def y_copy(direction, t):
        return remote(
            wown.at[t],
            w_slot(t, grp),
            y_send.at[direction, t],
            y_recv.at[direction, t],
            dev_yn if direction == 0 else dev_yp,
        )

    def yy_copy(t):
        g = grp_index(y_prev if t == 0 else y_next, xh, core)
        return remote(
            w_slot(t, g),
            w_slot(t, g),
            yy_send.at[t],
            yy_recv.at[t],
            dev_yn if t == 0 else dev_yp,
        )

    y_of = (y, y_prev, y_next, y_far)

    def wx_copy(i, t):
        g = grp_index(y_of[i], xh, core)
        return remote(
            wown.at[t] if i == 0 else w_slot(t, g),
            w_slot(t, g),
            wx_send.at[i, t],
            wx_recv.at[i, t],
            dev_xo,
        )

    def wc_copy(i, t):
        g = grp_index(y_of[i % 4], xh if i < 4 else 1 - xh, core)
        return remote(
            wown.at[t] if i == 0 else w_slot(t, g),
            w_slot(t, g),
            wc_send.at[i, t],
            wc_recv.at[i, t],
            dev_co,
        )

    x_pairs = (
        (give.at[0], kv.at[0, z, 1]),
        (give.at[1], kv.at[1, z, 1]),
        (qgive, qb.at[1]),
        (bias.at[0], bias.at[1]),
        (ogive.at[0], oin.at[0]),
        (ogive.at[1], oin.at[1]),
    )

    def x_copy(i):
        return remote(x_pairs[i][0], x_pairs[i][1], x_send.at[i], x_recv.at[i], dev_p)

    for p in range(2):
        local(6 * p).wait()
        local(6 * p + 1).wait()
        kv_copy(0, p, 0, 0).start()
        kv_copy(1, p, 0, 0).start()
        local(6 * p + 2).wait()
        local(6 * p + 3).wait()
        x_copy(p).start()
    local(5).wait()
    local(11).wait()
    x_copy(2).start()
    x_copy(3).start()
    local(13).wait()
    local(14).wait()
    for t in range(2):
        y_copy(0, t).start()
        y_copy(1, t).start()
        wx_copy(0, t).start()
        wc_copy(0, t).start()
        local(15 + t).start()
    for i in range(17, len(pairs)):
        local(i).start()
    for p in range(2):
        x_copy(p).wait_recv()
        kv_copy(0, p, 0, 1).start()
        kv_copy(1, p, 0, 1).start()
    local(4).wait()
    local(10).wait()
    x_copy(2).wait_recv()
    x_copy(3).wait_recv()

    lane = lax.broadcasted_iota(jnp.int32, (2 * BLK, BLK), 1)
    for h in range(LOCAL_HEADS):
        both = jnp.concatenate([qb[0, h // 2], qb[1, h // 2]], axis=0).astype(F32)
        keep = (lane < HD) if h % 2 == 0 else (lane >= HD)
        qz[h] = jnp.where(keep, both * (HD**-0.5), 0.0).astype(BF16)
    top[...] = jnp.full(top.shape, NEG, F32)
    total[...] = jnp.zeros(total.shape, F32)
    acc[...] = jnp.zeros(acc.shape, F32)

    def attend(slot, p):
        keys = jnp.concatenate([kv[p, slot, 0, 0], kv[p, slot, 1, 0]], axis=0)
        vals = jnp.concatenate([kv[p, slot, 0, 1], kv[p, slot, 1, 1]], axis=0)
        vals_t = jnp.transpose(vals)
        shift = []
        for j in range(2):
            block = slot * 2 + (xl if j == 0 else 1 - xl)
            shift.append(
                jnp.concatenate(
                    [bias[0, pl.ds(block, 1), :], bias[1, pl.ds(block, 1), :]], axis=1
                )
            )
        for u in range(2):
            h = 2 * p + u
            s = lax.dot_general(keys, qz[h], NT, preferred_element_type=F32)
            s0, s1 = s[:BLK], s[BLK:]
            old = top[h]
            new = jnp.maximum(
                jnp.max(s0, axis=0, keepdims=True) + shift[0],
                jnp.max(s1, axis=0, keepdims=True) + shift[1],
            )
            new = jnp.maximum(old, new)
            fade = jnp.exp(old - new)
            p0 = jnp.exp(s0 - (new - shift[0]))
            p1 = jnp.exp(s1 - (new - shift[1]))
            total[h] = (
                fade * total[h]
                + jnp.sum(p0, axis=0, keepdims=True)
                + jnp.sum(p1, axis=0, keepdims=True)
            )
            weight = jnp.concatenate([p0, p1], axis=0).astype(BF16)
            part = jnp.dot(
                vals_t[u * HD : (u + 1) * HD], weight, preferred_element_type=F32
            )
            acc[h] = acc[h] * fade + part
            top[h] = new

    def finish(p):
        out = jnp.concatenate(
            [acc[2 * p + u] * (1.0 / total[2 * p + u]) for u in range(2)], axis=0
        )
        out = jnp.transpose(out).astype(BF16)
        ogive[p] = out[BLK:]
        okeep[p] = out[:BLK]
        x_copy(4 + p).start()

    def project(value, side):
        return jnp.dot(
            jnp.concatenate([value[0], value[1]], axis=1),
            proj[pl.ds(pl.multiple_of(side * HALF, HALF), HALF), :],
            preferred_element_type=F32,
        )

    def w_first():
        for t in range(2):
            y_copy(0, t).wait_recv()
            y_copy(1, t).wait_recv()
        yy_copy(0).start()
        yy_copy(1).start()
        for i in (1, 2):
            for t in range(2):
                wx_copy(i, t).start()
                wc_copy(i, t).start()

    def w_second():
        for t in range(2):
            yy_copy(t).wait_recv()
            wx_copy(3, t).start()
            wc_copy(3, t).start()
        for t in range(2):
            wx_copy(0, t).wait_recv()
            wc_copy(4, t).start()

    def w_third():
        for i in (1, 2):
            for t in range(2):
                wx_copy(i, t).wait_recv()
                wc_copy(4 + i, t).start()

    def w_fourth():
        for t in range(2):
            wx_copy(3, t).wait_recv()
            wc_copy(7, t).start()

    def w_done():
        for i in range(8):
            for t in range(2):
                wc_copy(i, t).wait_recv()
        for i in range(15, 17):
            local(i).wait()
        for i in range(19, len(pairs)):
            local(i).wait()

    fb = w1_all.shape[0]
    portion = fb // 2

    def back_dact(first):
        def one(u, carry):
            c = first + u
            c0, c1 = cols_ref[0, c], cols_ref[1, c]
            gsel = jnp.concatenate([gblk[c0], gblk[c1]], axis=1)
            w2c = jnp.concatenate([w2_all[c, 0], w2_all[c, 1]], axis=1)
            dact_ref[c] = lax.dot_general(gsel, w2c, NT, preferred_element_type=F32)
            return carry

        lax.fori_loop(0, portion, one, 0)

    def step(d, carry):
        back = (z + nz - (d - 1)) % nz
        ahead = (z + d - 1) % nz
        more = d < half - 1

        for k, (j, p) in enumerate(((0, 0), (0, 1), (1, 0), (1, 1))):
            far_dir = j
            near_dir = 1 - j
            kv_landed(far_dir, p, d, j).wait_recv()
            kv_copy(far_dir, p, d, j).start()
            kv_landed(near_dir, p, d, j).wait_recv()

            @pl.when(more)
            def _(near_dir=near_dir, p=p, j=j):
                kv_copy(near_dir, p, d, j).start()

            if k < 2:
                attend(back, k)
            else:

                @pl.when(d > 1)
                def _(k=k):
                    attend(ahead, k - 2)

        pl.when(d == 1)(w_first)
        pl.when(d == 2)(w_second)
        pl.when(d == 4)(w_third)
        pl.when(d == 5)(w_fourth)
        pl.when(d == half - 2)(w_done)

        @pl.when(d > half - 3)
        def _():
            back_dact((d - half + 2) * portion)

        return carry

    lax.fori_loop(1, half, step, 0)

    def rest(i, carry):
        slot = jnp.where(i < 2, z + nz - (half - 1), z + half - 1) % nz
        attend(slot, i % 2)
        return carry

    lax.fori_loop(0, 4, rest, 0)
    local(17).wait()
    local(18).wait()
    for p in range(2):
        kv_landed(0, p, half, 0).wait_recv()
        kv_landed(1, p, half, 1).wait_recv()
        attend((z + half) % nz, p)
        finish(p)
    hidden_ref[...] = tokens[...].astype(F32) + project(okeep, xl)

    for t in range(2):
        y_copy(0, t).wait_send()
        y_copy(1, t).wait_send()
        yy_copy(t).wait_send()
        for i in range(4):
            wx_copy(i, t).wait_send()
        for i in range(8):
            wc_copy(i, t).wait_send()

    def drain(d, carry):
        for p in range(2):
            kv_copy(0, p, d, 0).wait_send()
            kv_copy(1, p, d, 1).wait_send()

        @pl.when(d < half - 1)
        def _():
            for p in range(2):
                kv_copy(0, p, d, 1).wait_send()
                kv_copy(1, p, d, 0).wait_send()

        return carry

    lax.fori_loop(0, half, drain, 0)
    for i in range(4):
        x_copy(i).wait_send()
    x_copy(4).wait()
    x_copy(5).wait()
    hidden_ref[...] += project(oin, 1 - xl)


def gather_attend(nz, ny, cols, query, key, value, mask, w1, w2, tokens, proj, gain, grad):
    hbm_spec = pl.BlockSpec(memory_space=pltpu.HBM)
    vmem_spec = pl.BlockSpec(memory_space=pltpu.VMEM)
    half = nz // 2
    db = D // BLK
    dma = pltpu.SemaphoreType.DMA
    fb = w1.shape[0] * ny * 4
    return pl.pallas_call(
        functools.partial(gather_attend_kernel, nz, ny),
        name="gather_attend",
        out_shape=(
            jax.ShapeDtypeStruct(tokens.shape, F32),
            jax.ShapeDtypeStruct((fb, BLK, BLK), F32),
            jax.ShapeDtypeStruct((db, BLK, BLK), BF16),
            jax.ShapeDtypeStruct(gain.shape, F32),
            jax.ShapeDtypeStruct((fb,) + w1.shape[1:], BF16),
            jax.ShapeDtypeStruct((fb,) + w2.shape[1:], BF16),
        ),
        in_specs=[hbm_spec] * 11,
        out_specs=(vmem_spec,) * 6,
        scratch_shapes=[
            pltpu.VMEM((2, nz, 2, 2, BLK, BLK), BF16),
            pltpu.VMEM((2, 2, BLK, BLK), BF16),
            pltpu.VMEM((2, 2, BLK, BLK), BF16),
            pltpu.VMEM((2, BLK, BLK), BF16),
            pltpu.VMEM((2,) + w1.shape, BF16),
            pltpu.SMEM(cols.shape, cols.dtype),
            pltpu.VMEM(mask.shape, mask.dtype),
            pltpu.VMEM(tokens.shape, BF16),
            pltpu.VMEM(proj.shape, BF16),
            pltpu.VMEM((2, 32, BLK), F32),
            pltpu.VMEM((LOCAL_HEADS, 2 * BLK, BLK), BF16),
            pltpu.VMEM((LOCAL_HEADS, 1, 2 * BLK), F32),
            pltpu.VMEM((LOCAL_HEADS, 1, 2 * BLK), F32),
            pltpu.VMEM((LOCAL_HEADS, HD, 2 * BLK), F32),
            pltpu.VMEM((2, BLK, BLK), BF16),
            pltpu.VMEM((2, BLK, BLK), BF16),
            pltpu.VMEM((2, BLK, BLK), BF16),
            dma((21 + db,)),
            dma((2, 2, half, 2)),
            dma((2, 2, half, 2)),
            dma((6,)),
            dma((6,)),
            dma((2, 2)),
            dma((2, 2)),
            dma((2,)),
            dma((2,)),
            dma((4, 2)),
            dma((4, 2)),
            dma((8, 2)),
            dma((8, 2)),
        ],
        compiler_params=pltpu.CompilerParams(
            collective_id=0, has_side_effects=True, vmem_limit_bytes=32 << 20
        ),
    )(
        *(
            pltpu.with_memory_space_constraint(x, pltpu.HBM)
            for x in (cols, query, key, value, mask, w1, w2, tokens, proj, gain, grad)
        ),
    )


def mlp_kernel(
    rows_ref,
    cols_ref,
    hidden_ref,
    dact_ref,
    gblk,
    gain_ref,
    w1,
    w2,
    out_ref,
    gin_ref,
    normed,
    xhat,
    mlp_acc,
    dn_acc,
    act,
    dpre,
):
    hidden = hidden_ref[...]
    mean = jnp.mean(hidden, axis=1, keepdims=True)
    removed = hidden - mean
    rstd = lax.rsqrt(jnp.mean(removed * removed, axis=1, keepdims=True) + 1e-06)
    unit = removed * rstd
    xhat[...] = unit
    normed_rows = (unit * gain_ref[...]).astype(BF16)
    db = D // BLK
    for b in range(db):
        cut = slice(b * BLK, (b + 1) * BLK)
        normed[b] = normed_rows[:, cut]
        mlp_acc[b] = hidden[:, cut]
        dn_acc[b] = jnp.zeros((BLK, BLK), F32)

    fb = w1.shape[0]
    group = 4

    def first(i, carry):
        for u in range(group):
            c = i * group + u
            picked = jnp.concatenate(
                [normed[rows_ref[0, c]], normed[rows_ref[1, c]]], axis=1
            )
            pre = jnp.dot(
                picked, w1[c].reshape(2 * BLK, BLK), preferred_element_type=F32
            )
            phi = 0.5 * (1.0 + lax.erf(pre * 0.7071067811865476))
            act[c] = (pre * phi).astype(BF16)
            slope = phi + pre * jnp.exp(-0.5 * pre * pre) * 0.3989422804014327
            dpre[c] = (dact_ref[c] * slope).astype(BF16)
        return carry

    lax.fori_loop(0, fb // group, first, 0)

    def second(i, carry):
        for u in range(group):
            c = i * group + u
            w2c = jnp.concatenate([w2[c, 0], w2[c, 1]], axis=1)
            fpart = jnp.dot(act[c], w2c, preferred_element_type=F32)
            mlp_acc[cols_ref[0, c]] += fpart[:, :BLK]
            mlp_acc[cols_ref[1, c]] += fpart[:, BLK:]
            bpart = lax.dot_general(
                dpre[c], w1[c].reshape(2 * BLK, BLK), NT, preferred_element_type=F32
            )
            dn_acc[rows_ref[0, c]] += bpart[:, :BLK]
            dn_acc[rows_ref[1, c]] += bpart[:, BLK:]
        return carry

    lax.fori_loop(0, fb // group, second, 0)

    for b in range(db):
        out_ref[:, b * BLK : (b + 1) * BLK] = mlp_acc[b].astype(BF16)
    dx = jnp.concatenate([dn_acc[b] for b in range(db)], axis=1) * gain_ref[...]
    unit = xhat[...]
    inner = (
        dx
        - jnp.mean(dx, axis=1, keepdims=True)
        - unit * jnp.mean(dx * unit, axis=1, keepdims=True)
    )
    grad = jnp.concatenate([gblk[b] for b in range(db)], axis=1)
    gin_ref[...] = (grad.astype(F32) + rstd * inner).astype(BF16)


def mlp_layer(rows, cols, hidden, dact, gblk, gain, w1, w2):
    vmem_spec = pl.BlockSpec(memory_space=pltpu.VMEM)
    smem_spec = pl.BlockSpec(memory_space=pltpu.SMEM)
    db = D // BLK
    fb = w1.shape[0]
    out = jax.ShapeDtypeStruct(hidden.shape, BF16)
    return pl.pallas_call(
        mlp_kernel,
        name="mlp_layer",
        out_shape=(out, out),
        in_specs=[smem_spec, smem_spec] + [vmem_spec] * 6,
        out_specs=(vmem_spec, vmem_spec),
        scratch_shapes=[
            pltpu.VMEM((db, BLK, BLK), BF16),
            pltpu.VMEM(hidden.shape, F32),
            pltpu.VMEM((db, BLK, BLK), F32),
            pltpu.VMEM((db, BLK, BLK), F32),
            pltpu.VMEM((fb, BLK, BLK), BF16),
            pltpu.VMEM((fb, BLK, BLK), BF16),
        ],
        compiler_params=pltpu.CompilerParams(vmem_limit_bytes=32 << 20),
    )(rows, cols, hidden, dact, gblk, gain, w1, w2)


def body(
    nz,
    ny,
    tokens,
    queries,
    keys,
    values,
    attn_mask,
    out_proj,
    norm_gain_vector,
    w1_packed,
    w1_rows,
    w2_packed,
    w2_cols,
    grad_out,
):
    rows, cols = w1_rows.T, w2_cols.T
    hidden, dact, gblk, gain, w1_all, w2_all = gather_attend(
        nz,
        ny,
        cols,
        queries[0],
        keys[0],
        values[0],
        attn_mask[0],
        w1_packed,
        w2_packed,
        tokens[0],
        out_proj,
        norm_gain_vector.reshape(1, D),
        grad_out[0],
    )
    out, gin = mlp_layer(rows, cols, hidden, dact, gblk, gain, w1_all, w2_all)
    return (out[None], gin[None])


def solution(mesh):
    nz = mesh.shape["seq"] // 2
    ny = mesh.shape["grp"] // 4
    return jax.shard_map(
        functools.partial(body, nz, ny),
        mesh=mesh,
        in_specs=(
            P("grp", "seq", None),
            P("grp", "seq", None),
            P("grp", "seq", None),
            P("grp", "seq", None),
            P("grp", "seq", None),
            P(),
            P(),
            P("grp", None, None, None),
            P(),
            P("grp", None, None, None),
            P(),
            P("grp", "seq", None),
        ),
        out_specs=(P("grp", "seq", None), P("grp", "seq", None)),
        check_vma=False,
    )
```

```python
import functools

import jax
import jax.numpy as jnp
from jax import lax
from jax.experimental import pallas as pl
from jax.experimental.pallas import tpu as pltpu
from jax.sharding import PartitionSpec as P

D = 1024
HD = 64
HEADS = 8
BLK = 128
HALF = 256
LOCAL_HEADS = 4
NEG = -1e30
BF16 = jnp.bfloat16
F32 = jnp.float32

NT = (((1,), (1,)), ((), ()))


def gather_attend_kernel(
    nz,
    ny,
    cols_hbm,
    q_hbm,
    k_hbm,
    v_hbm,
    mask_hbm,
    w1_hbm,
    w2_hbm,
    tokens_hbm,
    proj_hbm,
    gain_hbm,
    grad_hbm,
    hidden_ref,
    dact_ref,
    gblk,
    gain_ref,
    w1_all,
    w2_all,
    kv,
    qb,
    wown,
    cols_ref,
    mask,
    tokens,
    proj,
    bias,
    qz,
    top,
    total,
    acc,
    okeep,
    ogive,
    oin,
    loc,
    kv_send,
    kv_recv,
    x_send,
    x_recv,
    y_send,
    y_recv,
    yy_send,
    yy_recv,
    wx_send,
    wx_recv,
    wc_send,
    wc_recv,
):
    grp = lax.axis_index("grp")
    seq = lax.axis_index("seq")
    z = seq // 2
    xl = seq % 2
    y = grp // 4
    xh = (grp // 2) % 2
    core = grp % 2
    half = nz // 2
    db = D // BLK

    def seq_dev(zz, xx):
        return {"grp": grp, "seq": zz * 2 + xx}

    def grp_index(yy, hh, cc):
        return (yy * 2 + hh) * 2 + cc

    z_next = (z + 1) % nz
    z_prev = (z + nz - 1) % nz
    y_next = (y + 1) % ny
    y_prev = (y + ny - 1) % ny
    y_far = (y + 2) % ny
    dev_r = seq_dev(z_next, xl)
    dev_l = seq_dev(z_prev, xl)
    dev_p = seq_dev(z, 1 - xl)
    dev_yn = {"grp": grp_index(y_next, xh, core), "seq": seq}
    dev_yp = {"grp": grp_index(y_prev, xh, core), "seq": seq}
    dev_xo = {"grp": grp_index(y, 1 - xh, core), "seq": z * 2 + 1 - xl}
    dev_co = {"grp": grp_index(y, xh, 1 - core), "seq": seq}

    def columns(side, p):
        return pl.ds(pl.multiple_of(side * HALF + p * BLK, BLK), BLK)

    w_all = (w1_all, w2_all)

    pairs = []
    for p in range(2):
        pairs += [
            (k_hbm.at[:, columns(xl, p)], kv.at[p, z, 0, 0]),
            (v_hbm.at[:, columns(xl, p)], kv.at[p, z, 0, 1]),
            (q_hbm.at[:, columns(xl, p)], qb.at[0, p]),
        ]
    pairs += [
        (mask_hbm, mask),
        (w1_hbm, wown.at[0]),
        (w2_hbm, wown.at[1]),
        (wown.at[0], w1_all.at[pl.ds(2 * grp, 2)]),
        (wown.at[1], w2_all.at[pl.ds(2 * grp, 2)]),
        (tokens_hbm, tokens),
        (proj_hbm, proj),
        (gain_hbm, gain_ref),
        (cols_hbm, cols_ref),
    ]
    for b in range(db):
        pairs.append((grad_hbm.at[:, b * BLK : (b + 1) * BLK], gblk.at[b]))

    def local(i):
        return pltpu.make_async_copy(pairs[i][0], pairs[i][1], loc.at[i])

    def remote(src, dst, send, recv, device):
        return pltpu.make_async_remote_copy(
            src_ref=src,
            dst_ref=dst,
            send_sem=send,
            recv_sem=recv,
            device_id=device,
            device_id_type=pl.DeviceIdType.MESH,
        )

    barrier = pltpu.get_barrier_semaphore()
    for device in (dev_r, dev_l, dev_p, dev_yn, dev_yp, dev_xo, dev_co):
        pl.semaphore_signal(
            barrier, inc=1, device_id=device, device_id_type=pl.DeviceIdType.MESH
        )
    for i in (6, 7, 8, 0, 1, 2, 3, 4, 5):
        local(i).start()

    local(6).wait()
    rows = lax.broadcasted_iota(jnp.int32, (32, 32), 0)
    cols = lax.broadcasted_iota(jnp.int32, (32, 32), 1)
    seen = jnp.broadcast_to(mask[...].astype(F32), (32, 32))
    seen = jnp.sum(jnp.where(rows == cols, seen, 0.0), axis=1, keepdims=True)
    bias[0] = jnp.broadcast_to(jnp.where(seen == 1.0, 0.0, NEG), (32, BLK))
    pl.semaphore_wait(barrier, 7)

    def kv_slot(direction, d):
        return (z + nz - d) % nz if direction == 0 else (z + d) % nz

    def kv_copy(direction, p, d, j):
        here = kv.at[p, kv_slot(direction, d), j]
        return remote(
            here,
            here,
            kv_send.at[direction, p, d, j],
            kv_recv.at[direction, p, d, j],
            dev_r if direction == 0 else dev_l,
        )

    def kv_landed(direction, p, d, j):
        here = kv.at[p, kv_slot(direction, d), j]
        return remote(
            here,
            here,
            kv_send.at[direction, p, d - 1, j],
            kv_recv.at[direction, p, d - 1, j],
            dev_r if direction == 0 else dev_l,
        )

    def w_slot(t, g):
        return w_all[t].at[pl.ds(2 * g, 2)]

    def y_copy(direction, t):
        return remote(
            wown.at[t],
            w_slot(t, grp),
            y_send.at[direction, t],
            y_recv.at[direction, t],
            dev_yn if direction == 0 else dev_yp,
        )

    def yy_copy(t):
        g = grp_index(y_prev if t == 0 else y_next, xh, core)
        return remote(
            w_slot(t, g),
            w_slot(t, g),
            yy_send.at[t],
            yy_recv.at[t],
            dev_yn if t == 0 else dev_yp,
        )

    y_of = (y, y_prev, y_next, y_far)

    def wx_copy(i, t):
        g = grp_index(y_of[i], xh, core)
        return remote(
            wown.at[t] if i == 0 else w_slot(t, g),
            w_slot(t, g),
            wx_send.at[i, t],
            wx_recv.at[i, t],
            dev_xo,
        )

    def wc_copy(i, t):
        g = grp_index(y_of[i % 4], xh if i < 4 else 1 - xh, core)
        return remote(
            wown.at[t] if i == 0 else w_slot(t, g),
            w_slot(t, g),
            wc_send.at[i, t],
            wc_recv.at[i, t],
            dev_co,
        )

    x_pairs = (
        (kv.at[0, z, 0], kv.at[0, z, 1]),
        (kv.at[1, z, 0], kv.at[1, z, 1]),
        (qb.at[0], qb.at[1]),
        (bias.at[0], bias.at[1]),
        (ogive.at[0], oin.at[0]),
        (ogive.at[1], oin.at[1]),
    )

    def x_copy(i):
        return remote(x_pairs[i][0], x_pairs[i][1], x_send.at[i], x_recv.at[i], dev_p)

    kv_hbm = (k_hbm, v_hbm)
    for p in range(2):
        for direction in range(2):
            for i in range(2):
                remote(
                    kv_hbm[i].at[:, columns(xl, p)],
                    kv.at[p, z, 0, i],
                    kv_send.at[direction, p, 0, 0],
                    kv_recv.at[direction, p, 0, 0],
                    dev_r if direction == 0 else dev_l,
                ).start()
        for i in range(2):
            remote(
                kv_hbm[i].at[:, columns(1 - xl, p)],
                kv.at[p, z, 1, i],
                x_send.at[p],
                x_recv.at[p],
                dev_p,
            ).start()
    for p in range(2):
        remote(
            q_hbm.at[:, columns(1 - xl, p)],
            qb.at[1, p],
            x_send.at[2],
            x_recv.at[2],
            dev_p,
        ).start()
    x_copy(3).start()
    local(7).wait()
    local(8).wait()
    for t in range(2):
        y_copy(0, t).start()
        y_copy(1, t).start()
        wx_copy(0, t).start()
        wc_copy(0, t).start()
        local(9 + t).start()
    for p in range(2):
        x_copy(p).wait_recv()
        kv_copy(0, p, 0, 1).start()
        kv_copy(1, p, 0, 1).start()
    for i in range(11, len(pairs)):
        local(i).start()
    for i in range(6):
        local(i).wait()
    x_copy(2).wait_recv()
    x_copy(3).wait_recv()

    lane = lax.broadcasted_iota(jnp.int32, (2 * BLK, BLK), 1)
    for h in range(LOCAL_HEADS):
        both = jnp.concatenate([qb[0, h // 2], qb[1, h // 2]], axis=0).astype(F32)
        keep = (lane < HD) if h % 2 == 0 else (lane >= HD)
        qz[h] = jnp.where(keep, both * (HD**-0.5), 0.0).astype(BF16)
    top[...] = jnp.full(top.shape, NEG, F32)
    total[...] = jnp.zeros(total.shape, F32)
    acc[...] = jnp.zeros(acc.shape, F32)

    def attend(slot, p):
        keys = jnp.concatenate([kv[p, slot, 0, 0], kv[p, slot, 1, 0]], axis=0)
        vals = jnp.concatenate([kv[p, slot, 0, 1], kv[p, slot, 1, 1]], axis=0)
        vals_t = jnp.transpose(vals)
        shift = []
        for j in range(2):
            block = slot * 2 + (xl if j == 0 else 1 - xl)
            shift.append(
                jnp.concatenate(
                    [bias[0, pl.ds(block, 1), :], bias[1, pl.ds(block, 1), :]], axis=1
                )
            )
        cuts = (slice(0, BLK), slice(BLK, 2 * BLK))
        chains = [(u, cut) for u in range(2) for cut in cuts]
        state = [
            (top[2 * p + u][:, cut], total[2 * p + u][:, cut], acc[2 * p + u, :, cut])
            for u, cut in chains
        ]
        scores = [
            lax.dot_general(keys, qz[2 * p + u, cut], NT, preferred_element_type=F32)
            for u, cut in chains
        ]
        ready = []
        for (u, cut), (old, tot, part), s in zip(chains, state, scores):
            move = [x[:, cut] for x in shift]
            new = old
            for j in range(2):
                peak = jnp.max(s[j * BLK : (j + 1) * BLK], axis=0, keepdims=True)
                new = jnp.maximum(new, peak + move[j])
            fade = jnp.exp(old - new)
            tot = fade * tot
            weight = []
            for j in range(2):
                w = jnp.exp(s[j * BLK : (j + 1) * BLK] - (new - move[j]))
                tot = tot + jnp.sum(w, axis=0, keepdims=True)
                weight.append(w)
            weight = jnp.concatenate(weight, axis=0).astype(BF16)
            ready.append((new, tot, part * fade, weight))
        for (u, cut), (new, tot, part, weight) in zip(chains, ready):
            acc[2 * p + u, :, cut] = part + jnp.dot(
                vals_t[u * HD : (u + 1) * HD], weight, preferred_element_type=F32
            )
            top[2 * p + u, :, cut] = new
            total[2 * p + u, :, cut] = tot

    def finish(p):
        out = jnp.concatenate(
            [acc[2 * p + u] * (1.0 / total[2 * p + u]) for u in range(2)], axis=0
        )
        out = jnp.transpose(out).astype(BF16)
        ogive[p] = out[BLK:]
        okeep[p] = out[:BLK]
        x_copy(4 + p).start()

    def project(value, side):
        return jnp.dot(
            jnp.concatenate([value[0], value[1]], axis=1),
            proj[pl.ds(pl.multiple_of(side * HALF, HALF), HALF), :],
            preferred_element_type=F32,
        )

    def w_first():
        for t in range(2):
            y_copy(0, t).wait_recv()
            y_copy(1, t).wait_recv()
        yy_copy(0).start()
        yy_copy(1).start()
        for i in (1, 2):
            for t in range(2):
                wx_copy(i, t).start()
                wc_copy(i, t).start()

    def w_second():
        for t in range(2):
            yy_copy(t).wait_recv()
            wx_copy(3, t).start()
            wc_copy(3, t).start()
        for t in range(2):
            wx_copy(0, t).wait_recv()
            wc_copy(4, t).start()

    def w_third():
        for i in (1, 2):
            for t in range(2):
                wx_copy(i, t).wait_recv()
                wc_copy(4 + i, t).start()

    def w_fourth():
        for t in range(2):
            wx_copy(3, t).wait_recv()
            wc_copy(7, t).start()

    def w_done():
        for i in range(8):
            for t in range(2):
                wc_copy(i, t).wait_recv()
        for i in range(9, 11):
            local(i).wait()
        for i in range(13, len(pairs)):
            local(i).wait()

    fb = w1_all.shape[0]
    portion = fb // 4

    def back_dact(first):
        def one(u, carry):
            c = first + u
            c0, c1 = cols_ref[0, c], cols_ref[1, c]
            gsel = jnp.concatenate([gblk[c0], gblk[c1]], axis=1)
            w2c = jnp.concatenate([w2_all[c, 0], w2_all[c, 1]], axis=1)
            dact_ref[c] = lax.dot_general(gsel, w2c, NT, preferred_element_type=F32)
            return carry

        lax.fori_loop(0, portion, one, 0)

    def step(d, carry):
        back = (z + nz - d) % nz
        ahead = (z + d - 1) % nz
        more = d < half - 1

        for k, (j, p) in enumerate(((0, 0), (0, 1), (1, 0), (1, 1))):
            far_dir = j
            near_dir = 1 - j
            kv_landed(far_dir, p, d, j).wait_recv()
            kv_copy(far_dir, p, d, j).start()
            kv_landed(near_dir, p, d, j).wait_recv()

            @pl.when(more)
            def _(near_dir=near_dir, p=p, j=j):
                kv_copy(near_dir, p, d, j).start()

            if k == 0:
                pl.when(d == 5)(w_fourth)
            attend(ahead if k < 2 else back, p)

            @pl.when(d == half - 2)
            def _(k=k):
                back_dact(k * portion)

        pl.when(d == 1)(w_first)
        pl.when(d == 2)(w_second)
        pl.when(d == 4)(w_third)
        pl.when(d == 5)(w_done)
        return carry

    lax.fori_loop(1, half, step, 0)
    for p in range(2):
        attend((z + half - 1) % nz, p)
    local(11).wait()
    local(12).wait()
    for p in range(2):
        kv_landed(0, p, half, 0).wait_recv()
        kv_landed(1, p, half, 1).wait_recv()
        attend((z + half) % nz, p)
        finish(p)
    hidden_ref[...] = tokens[...].astype(F32) + project(okeep, xl)

    for t in range(2):
        y_copy(0, t).wait_send()
        y_copy(1, t).wait_send()
        yy_copy(t).wait_send()
        for i in range(4):
            wx_copy(i, t).wait_send()
        for i in range(8):
            wc_copy(i, t).wait_send()

    def drain(d, carry):
        for p in range(2):
            kv_copy(0, p, d, 0).wait_send()
            kv_copy(1, p, d, 1).wait_send()

        @pl.when(d < half - 1)
        def _():
            for p in range(2):
                kv_copy(0, p, d, 1).wait_send()
                kv_copy(1, p, d, 0).wait_send()

        return carry

    lax.fori_loop(0, half, drain, 0)
    for i in range(4):
        x_copy(i).wait_send()
    x_copy(4).wait()
    x_copy(5).wait()
    hidden_ref[...] += project(oin, 1 - xl)


def gather_attend(nz, ny, cols, query, key, value, mask, w1, w2, tokens, proj, gain, grad):
    hbm_spec = pl.BlockSpec(memory_space=pltpu.HBM)
    vmem_spec = pl.BlockSpec(memory_space=pltpu.VMEM)
    half = nz // 2
    db = D // BLK
    dma = pltpu.SemaphoreType.DMA
    fb = w1.shape[0] * ny * 4
    return pl.pallas_call(
        functools.partial(gather_attend_kernel, nz, ny),
        name="gather_attend",
        out_shape=(
            jax.ShapeDtypeStruct(tokens.shape, F32),
            jax.ShapeDtypeStruct((fb, BLK, BLK), F32),
            jax.ShapeDtypeStruct((db, BLK, BLK), BF16),
            jax.ShapeDtypeStruct(gain.shape, F32),
            jax.ShapeDtypeStruct((fb,) + w1.shape[1:], BF16),
            jax.ShapeDtypeStruct((fb,) + w2.shape[1:], BF16),
        ),
        in_specs=[hbm_spec] * 11,
        out_specs=(vmem_spec,) * 6,
        scratch_shapes=[
            pltpu.VMEM((2, nz, 2, 2, BLK, BLK), BF16),
            pltpu.VMEM((2, 2, BLK, BLK), BF16),
            pltpu.VMEM((2,) + w1.shape, BF16),
            pltpu.SMEM(cols.shape, cols.dtype),
            pltpu.VMEM(mask.shape, mask.dtype),
            pltpu.VMEM(tokens.shape, BF16),
            pltpu.VMEM(proj.shape, BF16),
            pltpu.VMEM((2, 32, BLK), F32),
            pltpu.VMEM((LOCAL_HEADS, 2 * BLK, BLK), BF16),
            pltpu.VMEM((LOCAL_HEADS, 1, 2 * BLK), F32),
            pltpu.VMEM((LOCAL_HEADS, 1, 2 * BLK), F32),
            pltpu.VMEM((LOCAL_HEADS, HD, 2 * BLK), F32),
            pltpu.VMEM((2, BLK, BLK), BF16),
            pltpu.VMEM((2, BLK, BLK), BF16),
            pltpu.VMEM((2, BLK, BLK), BF16),
            dma((15 + db,)),
            dma((2, 2, half, 2)),
            dma((2, 2, half, 2)),
            dma((6,)),
            dma((6,)),
            dma((2, 2)),
            dma((2, 2)),
            dma((2,)),
            dma((2,)),
            dma((4, 2)),
            dma((4, 2)),
            dma((8, 2)),
            dma((8, 2)),
        ],
        compiler_params=pltpu.CompilerParams(
            collective_id=0, has_side_effects=True, vmem_limit_bytes=32 << 20
        ),
    )(
        *(
            pltpu.with_memory_space_constraint(x, pltpu.HBM)
            for x in (cols, query, key, value, mask, w1, w2, tokens, proj, gain, grad)
        ),
    )


def mlp_kernel(
    rows_any,
    cols_any,
    hidden_ref,
    dact_ref,
    gblk,
    gain_ref,
    w1,
    w2,
    out_hbm,
    gin_hbm,
    rows_ref,
    cols_ref,
    out_ref,
    gin_ref,
    normed,
    xhat,
    mlp_acc,
    dn_acc,
    act,
    dpre,
    sems,
):
    tables = [
        pltpu.make_async_copy(rows_any, rows_ref, sems.at[0]),
        pltpu.make_async_copy(cols_any, cols_ref, sems.at[1]),
    ]
    for copy in tables:
        copy.start()
    hidden = hidden_ref[...]
    mean = jnp.mean(hidden, axis=1, keepdims=True)
    removed = hidden - mean
    rstd = lax.rsqrt(jnp.mean(removed * removed, axis=1, keepdims=True) + 1e-06)
    unit = removed * rstd
    xhat[...] = unit
    normed_rows = (unit * gain_ref[...]).astype(BF16)
    db = D // BLK
    for b in range(db):
        cut = slice(b * BLK, (b + 1) * BLK)
        normed[b] = normed_rows[:, cut]
        mlp_acc[b] = hidden[:, cut]
        dn_acc[b] = jnp.zeros((BLK, BLK), F32)
    for copy in tables:
        copy.wait()

    for c in range(w1.shape[0]):
        picked = jnp.concatenate(
            [normed[rows_ref[0, c]], normed[rows_ref[1, c]]], axis=1
        )
        pre = jnp.dot(picked, w1[c].reshape(2 * BLK, BLK), preferred_element_type=F32)
        phi = 0.5 * (1.0 + lax.erf(pre * 0.7071067811865476))
        act[c] = (pre * phi).astype(BF16)
        slope = phi + pre * jnp.exp(-0.5 * pre * pre) * 0.3989422804014327
        dpre[c] = (dact_ref[c] * slope).astype(BF16)

    for c in range(w1.shape[0]):
        w2c = jnp.concatenate([w2[c, 0], w2[c, 1]], axis=1)
        fpart = jnp.dot(act[c], w2c, preferred_element_type=F32)
        mlp_acc[cols_ref[0, c]] += fpart[:, :BLK]
        mlp_acc[cols_ref[1, c]] += fpart[:, BLK:]
        bpart = lax.dot_general(
            dpre[c], w1[c].reshape(2 * BLK, BLK), NT, preferred_element_type=F32
        )
        dn_acc[rows_ref[0, c]] += bpart[:, :BLK]
        dn_acc[rows_ref[1, c]] += bpart[:, BLK:]

    for b in range(db):
        out_ref[:, b * BLK : (b + 1) * BLK] = mlp_acc[b].astype(BF16)
    stores = [pltpu.make_async_copy(out_ref, out_hbm, sems.at[2])]
    stores[0].start()
    parts = 2
    size = BLK // parts
    for i in range(parts):
        some = slice(i * size, (i + 1) * size)
        dx = jnp.concatenate([dn_acc[b, some] for b in range(db)], axis=1)
        dx = dx * gain_ref[...]
        unit = xhat[some]
        inner = (
            dx
            - jnp.mean(dx, axis=1, keepdims=True)
            - unit * jnp.mean(dx * unit, axis=1, keepdims=True)
        )
        grad = jnp.concatenate([gblk[b, some] for b in range(db)], axis=1)
        gin_ref[some] = (grad.astype(F32) + rstd[some] * inner).astype(BF16)
        stores.append(
            pltpu.make_async_copy(gin_ref.at[some], gin_hbm.at[some], sems.at[3 + i])
        )
        stores[-1].start()
    for copy in stores:
        copy.wait()


def mlp_layer(rows, cols, hidden, dact, gblk, gain, w1, w2):
    vmem_spec = pl.BlockSpec(memory_space=pltpu.VMEM)
    any_spec = pl.BlockSpec(memory_space=pl.ANY)
    db = D // BLK
    fb = w1.shape[0]
    out = jax.ShapeDtypeStruct(hidden.shape, BF16)
    return pl.pallas_call(
        mlp_kernel,
        name="mlp_layer",
        out_shape=(out, out),
        in_specs=[any_spec, any_spec] + [vmem_spec] * 6,
        out_specs=(any_spec, any_spec),
        scratch_shapes=[
            pltpu.SMEM(rows.shape, rows.dtype),
            pltpu.SMEM(cols.shape, cols.dtype),
            pltpu.VMEM(hidden.shape, BF16),
            pltpu.VMEM(hidden.shape, BF16),
            pltpu.VMEM((db, BLK, BLK), BF16),
            pltpu.VMEM(hidden.shape, F32),
            pltpu.VMEM((db, BLK, BLK), F32),
            pltpu.VMEM((db, BLK, BLK), F32),
            pltpu.VMEM((fb, BLK, BLK), BF16),
            pltpu.VMEM((fb, BLK, BLK), BF16),
            pltpu.SemaphoreType.DMA((5,)),
        ],
        compiler_params=pltpu.CompilerParams(vmem_limit_bytes=32 << 20),
    )(rows, cols, hidden, dact, gblk, gain, w1, w2)


def body(
    nz,
    ny,
    tokens,
    queries,
    keys,
    values,
    attn_mask,
    out_proj,
    norm_gain_vector,
    w1_packed,
    w1_rows,
    w2_packed,
    w2_cols,
    grad_out,
):
    rows, cols = w1_rows.T, w2_cols.T
    hidden, dact, gblk, gain, w1_all, w2_all = gather_attend(
        nz,
        ny,
        cols,
        queries[0],
        keys[0],
        values[0],
        attn_mask[0],
        w1_packed,
        w2_packed,
        tokens[0],
        out_proj,
        norm_gain_vector.reshape(1, D),
        grad_out[0],
    )
    out, gin = mlp_layer(rows, cols, hidden, dact, gblk, gain, w1_all, w2_all)
    return (out[None], gin[None])


def solution(mesh):
    nz = mesh.shape["seq"] // 2
    ny = mesh.shape["grp"] // 4
    return jax.shard_map(
        functools.partial(body, nz, ny),
        mesh=mesh,
        in_specs=(
            P("grp", "seq", None),
            P("grp", "seq", None),
            P("grp", "seq", None),
            P("grp", "seq", None),
            P("grp", "seq", None),
            P(),
            P(),
            P("grp", None, None, None),
            P(),
            P("grp", None, None, None),
            P(),
            P("grp", "seq", None),
        ),
        out_specs=(P("grp", "seq", None), P("grp", "seq", None)),
        check_vma=False,
    )
```

```python
import functools

import jax
import jax.numpy as jnp
from jax import lax
from jax.experimental import pallas as pl
from jax.experimental.pallas import tpu as pltpu
from jax.sharding import PartitionSpec as P

D = 1024
HD = 64
HEADS = 8
BLK = 128
HALF = 256
LOCAL_HEADS = 4
NEG = -1e30
BF16 = jnp.bfloat16
F32 = jnp.float32

NT = (((1,), (1,)), ((), ()))


def gather_attend_kernel(
    nz,
    ny,
    cols_hbm,
    q_hbm,
    k_hbm,
    v_hbm,
    mask_hbm,
    w1_hbm,
    w2_hbm,
    tokens_hbm,
    proj_hbm,
    gain_hbm,
    grad_hbm,
    hidden_ref,
    dact_ref,
    gblk,
    gain_ref,
    w1_all,
    w2_all,
    kv,
    qb,
    wown,
    cols_ref,
    mask,
    tokens,
    proj,
    bias,
    qz,
    top,
    total,
    acc,
    okeep,
    ogive,
    oin,
    loc,
    kv_send,
    kv_recv,
    x_send,
    x_recv,
    y_send,
    y_recv,
    yy_send,
    yy_recv,
    wx_send,
    wx_recv,
    wc_send,
    wc_recv,
):
    grp = lax.axis_index("grp")
    seq = lax.axis_index("seq")
    z = seq // 2
    xl = seq % 2
    y = grp // 4
    xh = (grp // 2) % 2
    core = grp % 2
    half = nz // 2
    db = D // BLK

    def seq_dev(zz, xx):
        return {"grp": grp, "seq": zz * 2 + xx}

    def grp_index(yy, hh, cc):
        return (yy * 2 + hh) * 2 + cc

    z_next = (z + 1) % nz
    z_prev = (z + nz - 1) % nz
    y_next = (y + 1) % ny
    y_prev = (y + ny - 1) % ny
    y_far = (y + 2) % ny
    dev_r = seq_dev(z_next, xl)
    dev_l = seq_dev(z_prev, xl)
    dev_p = seq_dev(z, 1 - xl)
    dev_yn = {"grp": grp_index(y_next, xh, core), "seq": seq}
    dev_yp = {"grp": grp_index(y_prev, xh, core), "seq": seq}
    dev_xo = {"grp": grp_index(y, 1 - xh, core), "seq": z * 2 + 1 - xl}
    dev_co = {"grp": grp_index(y, xh, 1 - core), "seq": seq}

    def columns(side, p):
        return pl.ds(pl.multiple_of(side * HALF + p * BLK, BLK), BLK)

    w_all = (w1_all, w2_all)

    pairs = []
    for p in range(2):
        pairs += [
            (k_hbm.at[:, columns(xl, p)], kv.at[p, z, 0, 0]),
            (v_hbm.at[:, columns(xl, p)], kv.at[p, z, 0, 1]),
            (q_hbm.at[:, columns(xl, p)], qb.at[0, p]),
        ]
    pairs += [
        (mask_hbm, mask),
        (w1_hbm, wown.at[0]),
        (w2_hbm, wown.at[1]),
        (wown.at[0], w1_all.at[pl.ds(2 * grp, 2)]),
        (wown.at[1], w2_all.at[pl.ds(2 * grp, 2)]),
        (tokens_hbm, tokens),
        (proj_hbm, proj),
        (gain_hbm, gain_ref),
        (cols_hbm, cols_ref),
    ]
    for b in range(db):
        pairs.append((grad_hbm.at[:, b * BLK : (b + 1) * BLK], gblk.at[b]))

    def local(i):
        return pltpu.make_async_copy(pairs[i][0], pairs[i][1], loc.at[i])

    def remote(src, dst, send, recv, device):
        return pltpu.make_async_remote_copy(
            src_ref=src,
            dst_ref=dst,
            send_sem=send,
            recv_sem=recv,
            device_id=device,
            device_id_type=pl.DeviceIdType.MESH,
        )

    barrier = pltpu.get_barrier_semaphore()
    for device in (dev_r, dev_l, dev_p, dev_yn, dev_yp, dev_xo, dev_co):
        pl.semaphore_signal(
            barrier, inc=1, device_id=device, device_id_type=pl.DeviceIdType.MESH
        )
    for i in (6, 7, 8, 0, 1, 2, 3, 4, 5):
        local(i).start()

    local(6).wait()
    rows = lax.broadcasted_iota(jnp.int32, (32, 32), 0)
    cols = lax.broadcasted_iota(jnp.int32, (32, 32), 1)
    seen = jnp.broadcast_to(mask[...].astype(F32), (32, 32))
    seen = jnp.sum(jnp.where(rows == cols, seen, 0.0), axis=1, keepdims=True)
    bias[0] = jnp.broadcast_to(jnp.where(seen == 1.0, 0.0, NEG), (32, BLK))
    pl.semaphore_wait(barrier, 7)

    def kv_slot(direction, d):
        return (z + nz - d) % nz if direction == 0 else (z + d) % nz

    def kv_copy(direction, p, d, j):
        here = kv.at[p, kv_slot(direction, d), j]
        return remote(
            here,
            here,
            kv_send.at[direction, p, d, j],
            kv_recv.at[direction, p, d, j],
            dev_r if direction == 0 else dev_l,
        )

    def kv_landed(direction, p, d, j):
        here = kv.at[p, kv_slot(direction, d), j]
        return remote(
            here,
            here,
            kv_send.at[direction, p, d - 1, j],
            kv_recv.at[direction, p, d - 1, j],
            dev_r if direction == 0 else dev_l,
        )

    def w_slot(t, g):
        return w_all[t].at[pl.ds(2 * g, 2)]

    def y_copy(direction, t):
        return remote(
            wown.at[t],
            w_slot(t, grp),
            y_send.at[direction, t],
            y_recv.at[direction, t],
            dev_yn if direction == 0 else dev_yp,
        )

    def yy_copy(t):
        g = grp_index(y_prev if t == 0 else y_next, xh, core)
        return remote(
            w_slot(t, g),
            w_slot(t, g),
            yy_send.at[t],
            yy_recv.at[t],
            dev_yn if t == 0 else dev_yp,
        )

    y_of = (y, y_prev, y_next, y_far)

    def wx_copy(i, t):
        g = grp_index(y_of[i], xh, core)
        return remote(
            wown.at[t] if i == 0 else w_slot(t, g),
            w_slot(t, g),
            wx_send.at[i, t],
            wx_recv.at[i, t],
            dev_xo,
        )

    def wc_copy(i, t):
        g = grp_index(y_of[i % 4], xh if i < 4 else 1 - xh, core)
        return remote(
            wown.at[t] if i == 0 else w_slot(t, g),
            w_slot(t, g),
            wc_send.at[i, t],
            wc_recv.at[i, t],
            dev_co,
        )

    x_pairs = (
        (kv.at[0, z, 0], kv.at[0, z, 1]),
        (kv.at[1, z, 0], kv.at[1, z, 1]),
        (qb.at[0], qb.at[1]),
        (bias.at[0], bias.at[1]),
        (ogive.at[0], oin.at[0]),
        (ogive.at[1], oin.at[1]),
    )

    def x_copy(i):
        return remote(x_pairs[i][0], x_pairs[i][1], x_send.at[i], x_recv.at[i], dev_p)

    kv_hbm = (k_hbm, v_hbm)
    for p in range(2):
        for direction in range(2):
            for i in range(2):
                remote(
                    kv_hbm[i].at[:, columns(xl, p)],
                    kv.at[p, z, 0, i],
                    kv_send.at[direction, p, 0, 0],
                    kv_recv.at[direction, p, 0, 0],
                    dev_r if direction == 0 else dev_l,
                ).start()
        for i in range(2):
            remote(
                kv_hbm[i].at[:, columns(1 - xl, p)],
                kv.at[p, z, 1, i],
                x_send.at[p],
                x_recv.at[p],
                dev_p,
            ).start()
    for p in range(2):
        remote(
            q_hbm.at[:, columns(1 - xl, p)],
            qb.at[1, p],
            x_send.at[2],
            x_recv.at[2],
            dev_p,
        ).start()
    x_copy(3).start()
    local(7).wait()
    local(8).wait()
    for t in range(2):
        y_copy(0, t).start()
        y_copy(1, t).start()
        wx_copy(0, t).start()
        wc_copy(0, t).start()
        local(9 + t).start()
    for p in range(2):
        x_copy(p).wait_recv()
        kv_copy(0, p, 0, 1).start()
        kv_copy(1, p, 0, 1).start()
    for i in range(11, len(pairs)):
        local(i).start()
    for i in range(6):
        local(i).wait()
    x_copy(2).wait_recv()
    x_copy(3).wait_recv()

    lane = lax.broadcasted_iota(jnp.int32, (2 * BLK, BLK), 1)
    for h in range(LOCAL_HEADS):
        both = jnp.concatenate([qb[0, h // 2], qb[1, h // 2]], axis=0).astype(F32)
        keep = (lane < HD) if h % 2 == 0 else (lane >= HD)
        qz[h] = jnp.where(keep, both * (HD**-0.5), 0.0).astype(BF16)
    top[...] = jnp.full(top.shape, NEG, F32)
    total[...] = jnp.zeros(total.shape, F32)
    acc[...] = jnp.zeros(acc.shape, F32)

    def attend(slot, p):
        keys = jnp.concatenate([kv[p, slot, 0, 0], kv[p, slot, 1, 0]], axis=0)
        vals = jnp.concatenate([kv[p, slot, 0, 1], kv[p, slot, 1, 1]], axis=0)
        vals_t = jnp.transpose(vals)
        shift = []
        for j in range(2):
            block = slot * 2 + (xl if j == 0 else 1 - xl)
            shift.append(
                jnp.concatenate(
                    [bias[0, pl.ds(block, 1), :], bias[1, pl.ds(block, 1), :]], axis=1
                )
            )
        cuts = (slice(0, BLK), slice(BLK, 2 * BLK))
        chains = [(u, cut) for u in range(2) for cut in cuts]
        state = [
            (top[2 * p + u][:, cut], total[2 * p + u][:, cut], acc[2 * p + u, :, cut])
            for u, cut in chains
        ]
        scores = [
            lax.dot_general(keys, qz[2 * p + u, cut], NT, preferred_element_type=F32)
            for u, cut in chains
        ]
        ready = []
        for (u, cut), (old, tot, part), s in zip(chains, state, scores):
            move = [x[:, cut] for x in shift]
            new = old
            for j in range(2):
                peak = jnp.max(s[j * BLK : (j + 1) * BLK], axis=0, keepdims=True)
                new = jnp.maximum(new, peak + move[j])
            fade = jnp.exp(old - new)
            tot = fade * tot
            weight = []
            for j in range(2):
                w = jnp.exp(s[j * BLK : (j + 1) * BLK] - (new - move[j]))
                tot = tot + jnp.sum(w, axis=0, keepdims=True)
                weight.append(w)
            weight = jnp.concatenate(weight, axis=0).astype(BF16)
            ready.append((new, tot, part * fade, weight))
        for (u, cut), (new, tot, part, weight) in zip(chains, ready):
            acc[2 * p + u, :, cut] = part + jnp.dot(
                vals_t[u * HD : (u + 1) * HD], weight, preferred_element_type=F32
            )
            top[2 * p + u, :, cut] = new
            total[2 * p + u, :, cut] = tot

    def finish(p):
        out = jnp.concatenate(
            [acc[2 * p + u] * (1.0 / total[2 * p + u]) for u in range(2)], axis=0
        )
        out = jnp.transpose(out).astype(BF16)
        ogive[p] = out[BLK:]
        okeep[p] = out[:BLK]
        x_copy(4 + p).start()

    def project(value, side):
        return jnp.dot(
            jnp.concatenate([value[0], value[1]], axis=1),
            proj[pl.ds(pl.multiple_of(side * HALF, HALF), HALF), :],
            preferred_element_type=F32,
        )

    def w_first():
        for t in range(2):
            y_copy(0, t).wait_recv()
            y_copy(1, t).wait_recv()
        yy_copy(0).start()
        yy_copy(1).start()
        for i in (1, 2):
            for t in range(2):
                wx_copy(i, t).start()
                wc_copy(i, t).start()

    def w_second():
        for t in range(2):
            yy_copy(t).wait_recv()
            wx_copy(3, t).start()
            wc_copy(3, t).start()
        for t in range(2):
            wx_copy(0, t).wait_recv()
            wc_copy(4, t).start()

    def w_third():
        for i in (1, 2):
            for t in range(2):
                wx_copy(i, t).wait_recv()
                wc_copy(4 + i, t).start()

    def w_fourth():
        for t in range(2):
            wx_copy(3, t).wait_recv()
            wc_copy(7, t).start()

    def w_done():
        for i in range(8):
            for t in range(2):
                wc_copy(i, t).wait_recv()
        for i in range(9, 11):
            local(i).wait()
        for i in range(13, len(pairs)):
            local(i).wait()

    fb = w1_all.shape[0]
    portion = fb // 4

    def back_dact(first):
        for u in range(portion):
            c = first + u
            c0, c1 = cols_ref[0, c], cols_ref[1, c]
            gsel = jnp.concatenate([gblk[c0], gblk[c1]], axis=1)
            w2c = jnp.concatenate([w2_all[c, 0], w2_all[c, 1]], axis=1)
            dact_ref[c] = lax.dot_general(gsel, w2c, NT, preferred_element_type=F32)

    def step(d, carry):
        back = (z + nz - d) % nz
        ahead = (z + d - 1) % nz
        more = d < half - 1

        for k, (j, p) in enumerate(((0, 0), (0, 1), (1, 0), (1, 1))):
            far_dir = j
            near_dir = 1 - j
            kv_landed(far_dir, p, d, j).wait_recv()
            kv_copy(far_dir, p, d, j).start()
            kv_landed(near_dir, p, d, j).wait_recv()

            @pl.when(more)
            def _(near_dir=near_dir, p=p, j=j):
                kv_copy(near_dir, p, d, j).start()

            if k == 0:
                pl.when(d == 5)(w_fourth)
            attend(ahead if k < 2 else back, p)

            @pl.when(d == half - 2)
            def _(k=k):
                back_dact(k * portion)

        pl.when(d == 1)(w_first)
        pl.when(d == 2)(w_second)
        pl.when(d == 4)(w_third)
        pl.when(d == 5)(w_done)
        return carry

    lax.fori_loop(1, half, step, 0)
    for p in range(2):
        attend((z + half - 1) % nz, p)
    local(11).wait()
    local(12).wait()
    for p in range(2):
        kv_landed(0, p, half, 0).wait_recv()
        kv_landed(1, p, half, 1).wait_recv()
        attend((z + half) % nz, p)
        finish(p)
    hidden_ref[...] = tokens[...].astype(F32) + project(okeep, xl)

    for t in range(2):
        y_copy(0, t).wait_send()
        y_copy(1, t).wait_send()
        yy_copy(t).wait_send()
        for i in range(4):
            wx_copy(i, t).wait_send()
        for i in range(8):
            wc_copy(i, t).wait_send()

    def drain(d, carry):
        for p in range(2):
            kv_copy(0, p, d, 0).wait_send()
            kv_copy(1, p, d, 1).wait_send()

        @pl.when(d < half - 1)
        def _():
            for p in range(2):
                kv_copy(0, p, d, 1).wait_send()
                kv_copy(1, p, d, 0).wait_send()

        return carry

    lax.fori_loop(0, half, drain, 0)
    for i in range(4):
        x_copy(i).wait_send()
    x_copy(4).wait()
    x_copy(5).wait()
    hidden_ref[...] += project(oin, 1 - xl)


def gather_attend(nz, ny, cols, query, key, value, mask, w1, w2, tokens, proj, gain, grad):
    hbm_spec = pl.BlockSpec(memory_space=pltpu.HBM)
    vmem_spec = pl.BlockSpec(memory_space=pltpu.VMEM)
    half = nz // 2
    db = D // BLK
    dma = pltpu.SemaphoreType.DMA
    fb = w1.shape[0] * ny * 4
    return pl.pallas_call(
        functools.partial(gather_attend_kernel, nz, ny),
        name="gather_attend",
        out_shape=(
            jax.ShapeDtypeStruct(tokens.shape, F32),
            jax.ShapeDtypeStruct((fb, BLK, BLK), F32),
            jax.ShapeDtypeStruct((db, BLK, BLK), BF16),
            jax.ShapeDtypeStruct(gain.shape, F32),
            jax.ShapeDtypeStruct((fb,) + w1.shape[1:], BF16),
            jax.ShapeDtypeStruct((fb,) + w2.shape[1:], BF16),
        ),
        in_specs=[hbm_spec] * 11,
        out_specs=(vmem_spec,) * 6,
        scratch_shapes=[
            pltpu.VMEM((2, nz, 2, 2, BLK, BLK), BF16),
            pltpu.VMEM((2, 2, BLK, BLK), BF16),
            pltpu.VMEM((2,) + w1.shape, BF16),
            pltpu.SMEM(cols.shape, cols.dtype),
            pltpu.VMEM(mask.shape, mask.dtype),
            pltpu.VMEM(tokens.shape, BF16),
            pltpu.VMEM(proj.shape, BF16),
            pltpu.VMEM((2, 32, BLK), F32),
            pltpu.VMEM((LOCAL_HEADS, 2 * BLK, BLK), BF16),
            pltpu.VMEM((LOCAL_HEADS, 1, 2 * BLK), F32),
            pltpu.VMEM((LOCAL_HEADS, 1, 2 * BLK), F32),
            pltpu.VMEM((LOCAL_HEADS, HD, 2 * BLK), F32),
            pltpu.VMEM((2, BLK, BLK), BF16),
            pltpu.VMEM((2, BLK, BLK), BF16),
            pltpu.VMEM((2, BLK, BLK), BF16),
            dma((15 + db,)),
            dma((2, 2, half, 2)),
            dma((2, 2, half, 2)),
            dma((6,)),
            dma((6,)),
            dma((2, 2)),
            dma((2, 2)),
            dma((2,)),
            dma((2,)),
            dma((4, 2)),
            dma((4, 2)),
            dma((8, 2)),
            dma((8, 2)),
        ],
        compiler_params=pltpu.CompilerParams(
            collective_id=0, has_side_effects=True, vmem_limit_bytes=32 << 20
        ),
    )(
        *(
            pltpu.with_memory_space_constraint(x, pltpu.HBM)
            for x in (cols, query, key, value, mask, w1, w2, tokens, proj, gain, grad)
        ),
    )


def mlp_kernel(
    rows_any,
    cols_any,
    hidden_ref,
    dact_ref,
    gblk,
    gain_ref,
    w1,
    w2,
    out_hbm,
    gin_hbm,
    rows_ref,
    cols_ref,
    out_ref,
    gin_ref,
    normed,
    xhat,
    mlp_acc,
    dn_acc,
    act,
    dpre,
    sems,
):
    tables = [
        pltpu.make_async_copy(rows_any, rows_ref, sems.at[0]),
        pltpu.make_async_copy(cols_any, cols_ref, sems.at[1]),
    ]
    for copy in tables:
        copy.start()
    hidden = hidden_ref[...]
    mean = jnp.mean(hidden, axis=1, keepdims=True)
    removed = hidden - mean
    rstd = lax.rsqrt(jnp.mean(removed * removed, axis=1, keepdims=True) + 1e-06)
    unit = removed * rstd
    xhat[...] = unit
    normed_rows = (unit * gain_ref[...]).astype(BF16)
    db = D // BLK
    for b in range(db):
        cut = slice(b * BLK, (b + 1) * BLK)
        normed[b] = normed_rows[:, cut]
        mlp_acc[b] = hidden[:, cut]
        dn_acc[b] = jnp.zeros((BLK, BLK), F32)
    for copy in tables:
        copy.wait()

    fb = w1.shape[0]
    skew = 4

    def first(c):
        picked = jnp.concatenate(
            [normed[rows_ref[0, c]], normed[rows_ref[1, c]]], axis=1
        )
        pre = jnp.dot(picked, w1[c].reshape(2 * BLK, BLK), preferred_element_type=F32)
        phi = 0.5 * (1.0 + lax.erf(pre * 0.7071067811865476))
        act[c] = (pre * phi).astype(BF16)
        slope = phi + pre * jnp.exp(-0.5 * pre * pre) * 0.3989422804014327
        dpre[c] = (dact_ref[c] * slope).astype(BF16)

    def second(c):
        w2c = jnp.concatenate([w2[c, 0], w2[c, 1]], axis=1)
        fpart = jnp.dot(act[c], w2c, preferred_element_type=F32)
        bpart = lax.dot_general(
            dpre[c], w1[c].reshape(2 * BLK, BLK), NT, preferred_element_type=F32
        )
        for n in range(2):
            cut = slice(n * BLK, (n + 1) * BLK)
            mlp_acc[cols_ref[n, c]] += fpart[:, cut]
            dn_acc[rows_ref[n, c]] += bpart[:, cut]

    for c in range(fb + skew):
        if c < fb:
            first(c)
        if c >= skew:
            second(c - skew)

    for b in range(db):
        out_ref[:, b * BLK : (b + 1) * BLK] = mlp_acc[b].astype(BF16)
    stores = [pltpu.make_async_copy(out_ref, out_hbm, sems.at[2])]
    stores[0].start()
    parts = 2
    size = BLK // parts
    for i in range(parts):
        some = slice(i * size, (i + 1) * size)
        dx = jnp.concatenate([dn_acc[b, some] for b in range(db)], axis=1)
        dx = dx * gain_ref[...]
        unit = xhat[some]
        inner = (
            dx
            - jnp.mean(dx, axis=1, keepdims=True)
            - unit * jnp.mean(dx * unit, axis=1, keepdims=True)
        )
        grad = jnp.concatenate([gblk[b, some] for b in range(db)], axis=1)
        gin_ref[some] = (grad.astype(F32) + rstd[some] * inner).astype(BF16)
        stores.append(
            pltpu.make_async_copy(gin_ref.at[some], gin_hbm.at[some], sems.at[3 + i])
        )
        stores[-1].start()
    for copy in stores:
        copy.wait()


def mlp_layer(rows, cols, hidden, dact, gblk, gain, w1, w2):
    vmem_spec = pl.BlockSpec(memory_space=pltpu.VMEM)
    any_spec = pl.BlockSpec(memory_space=pl.ANY)
    db = D // BLK
    fb = w1.shape[0]
    out = jax.ShapeDtypeStruct(hidden.shape, BF16)
    return pl.pallas_call(
        mlp_kernel,
        name="mlp_layer",
        out_shape=(out, out),
        in_specs=[any_spec, any_spec] + [vmem_spec] * 6,
        out_specs=(any_spec, any_spec),
        scratch_shapes=[
            pltpu.SMEM(rows.shape, rows.dtype),
            pltpu.SMEM(cols.shape, cols.dtype),
            pltpu.VMEM(hidden.shape, BF16),
            pltpu.VMEM(hidden.shape, BF16),
            pltpu.VMEM((db, BLK, BLK), BF16),
            pltpu.VMEM(hidden.shape, F32),
            pltpu.VMEM((db, BLK, BLK), F32),
            pltpu.VMEM((db, BLK, BLK), F32),
            pltpu.VMEM((fb, BLK, BLK), BF16),
            pltpu.VMEM((fb, BLK, BLK), BF16),
            pltpu.SemaphoreType.DMA((5,)),
        ],
        compiler_params=pltpu.CompilerParams(vmem_limit_bytes=32 << 20),
    )(rows, cols, hidden, dact, gblk, gain, w1, w2)


def body(
    nz,
    ny,
    tokens,
    queries,
    keys,
    values,
    attn_mask,
    out_proj,
    norm_gain_vector,
    w1_packed,
    w1_rows,
    w2_packed,
    w2_cols,
    grad_out,
):
    rows, cols = w1_rows.T, w2_cols.T
    hidden, dact, gblk, gain, w1_all, w2_all = gather_attend(
        nz,
        ny,
        cols,
        queries[0],
        keys[0],
        values[0],
        attn_mask[0],
        w1_packed,
        w2_packed,
        tokens[0],
        out_proj,
        norm_gain_vector.reshape(1, D),
        grad_out[0],
    )
    out, gin = mlp_layer(rows, cols, hidden, dact, gblk, gain, w1_all, w2_all)
    return (out[None], gin[None])


def solution(mesh):
    nz = mesh.shape["seq"] // 2
    ny = mesh.shape["grp"] // 4
    return jax.shard_map(
        functools.partial(body, nz, ny),
        mesh=mesh,
        in_specs=(
            P("grp", "seq", None),
            P("grp", "seq", None),
            P("grp", "seq", None),
            P("grp", "seq", None),
            P("grp", "seq", None),
            P(),
            P(),
            P("grp", None, None, None),
            P(),
            P("grp", None, None, None),
            P(),
            P("grp", "seq", None),
        ),
        out_specs=(P("grp", "seq", None), P("grp", "seq", None)),
        check_vma=False,
    )
```
